32 devices in a mesh: gx: 4 (over y, core), gy: 4 (over z), gz: 2 (over x).
Axes of the slice: x: 2, y: 2, z: 4, core: 2. Of those that a mesh axis runs over, the one named last changes fastest.
Arguments:
- positions: float32 [4, 16, 2, 3, 128], P('gx', 'gy', 'gz'), may hold values from 0 to 1
- velocities: float32 [4, 16, 2, 3, 128], P('gx', 'gy', 'gz'), may hold values from -6 to 6
- charges: float32 [4, 16, 2, 128], P('gx', 'gy', 'gz'), may hold values from -3 to 3
- atom_types: int32 [4, 16, 2, 128], P('gx', 'gy', 'gz'), may hold values from 0 to 15
- atom_count: int32 [4, 16, 2], P('gx', 'gy', 'gz'), may hold values from 32 to 128
- sigma_type: float32 [16], replicated, may hold values from 0.15 to 0.35
- epsilon_type: float32 [16], replicated, may hold values from 0.3 to 3
- masses: float32 [4, 16, 2, 128], P('gx', 'gy', 'gz'), may hold values from 1 to 4
- pair_list: int32 [4, 4, 2, 2, 56], P('gx', 'gy', 'gz'), may hold values from 0 to 19, as said below
- pair_count: int32 [4, 4, 2], P('gx', 'gy', 'gz'), may hold values from 1 to 56, as said below
- pos_cotangent: float32 [4, 16, 2, 3, 128], P('gx', 'gy', 'gz'), may hold values from -6 to 6
- vel_cotangent: float32 [4, 16, 2, 3, 128], P('gx', 'gy', 'gz'), may hold values from -6 to 6
Outputs:
- pos_final: float32 [4, 16, 2, 3, 128], P('gx', 'gy', 'gz')
- vel_final: float32 [4, 16, 2, 3, 128], P('gx', 'gy', 'gz')
- grad_pos: float32 [4, 16, 2, 3, 128], P('gx', 'gy', 'gz')
- grad_vel: float32 [4, 16, 2, 3, 128], P('gx', 'gy', 'gz')
- grad_charge: float32 [4, 16, 2, 128], P('gx', 'gy', 'gz')
The draws below stay inside these ranges and needn't reach their ends.
Inputs may be any that keep to these rules, and one draw needn't show every extreme that they name: `pair_list`: for k < pair_count[a, b, c] the two extended indices of slot k name blocks inside the global grid of 4 x 16 x 2 blocks, their coordinates differ by at most one in each dimension, and their smaller coordinate in each dimension lies in the device's own blocks; an unordered pair of blocks appears in at most one live slot over all devices. Slots at and past the count hold indices in range and are ignored. `pair_count`: some device has all 56 slots live in every draw.
All inputs are finite; a program needn't handle non-finite values.
Results may differ from the reference program's by a relative error of at most 0.00027.
Values sent between devices are 32-bit elements; how exact they have to be, the bound alone decides.
A program may use at most 64 MiB of HBM per device.

```python
import math
import jax
import jax.numpy as jnp
import numpy as np
from jax import lax

BX = 1
BY = 4
BZ = 1
ATOMS = 128
NTYPES = 16
STEPS = 5
NX = 4
NY = 16
NZ = 2


def corner_pairs():
    options = ((0, 0), (0, 1), (1, 0))
    lefts = []
    rights = []
    for option_x in options:
        for option_y in options:
            for option_z in options:
                left_corner = (option_x[0], option_y[0], option_z[0])
                right_corner = (option_x[1], option_y[1], option_z[1])
                if left_corner <= right_corner:
                    lefts.append(left_corner)
                    rights.append(right_corner)
    return (np.array(lefts, dtype=np.int32), np.array(rights, dtype=np.int32))


def pair_tables(key):
    grid_x = NX // BX
    grid_y = NY // BY
    grid_z = NZ // BZ
    lefts, rights = corner_pairs()
    own_cells = np.array([[cell_x, cell_y, cell_z] for cell_x in range(BX) for cell_y in range(BY) for cell_z in range(BZ)], dtype=np.int32)
    cand_left = (own_cells[:, None, :] + lefts[None, :, :]).reshape(-1, 3)
    cand_right = (own_cells[:, None, :] + rights[None, :, :]).reshape(-1, 3)
    slot_total = cand_left.shape[0]

    def ext_index(coords):
        return ((coords[:, 0] * (BY + 1) + coords[:, 1]) * (BZ + 1) + coords[:, 2]).astype(np.int32)
    anchors = np.array([[dev_x * BX, dev_y * BY, dev_z * BZ] for dev_x in range(grid_x) for dev_y in range(grid_y) for dev_z in range(grid_z)], dtype=np.int32)
    highest = jnp.maximum(jnp.asarray(cand_left), jnp.asarray(cand_right))
    limits = jnp.asarray(np.array([NX, NY, NZ], dtype=np.int32))
    inside = jnp.all(jnp.asarray(anchors)[:, None, :] + highest[None, :, :] < limits, axis=-1)
    inside_total = jnp.sum(inside.astype(jnp.int32), axis=1).astype(jnp.int32)
    device_total = anchors.shape[0]
    shuffled = jax.vmap(lambda sub_key: jax.random.permutation(sub_key, slot_total))(jax.random.split(jax.random.fold_in(key, 11), device_total))
    scores = (jnp.where(inside, 0, slot_total) + shuffled).astype(jnp.int32)
    ordering = jnp.argsort(scores, axis=1, stable=True)
    left_ids = jnp.asarray(ext_index(cand_left))[ordering]
    right_ids = jnp.asarray(ext_index(cand_right))[ordering]
    reversal = jax.random.randint(jax.random.fold_in(key, 12), (device_total, slot_total), 0, 2)
    firsts = jnp.where(reversal == 1, right_ids, left_ids)
    seconds = jnp.where(reversal == 1, left_ids, right_ids)
    levels = jax.random.randint(jax.random.fold_in(key, 13), (device_total,), 1, 9)
    counts = jnp.maximum(slot_total * levels * levels // 64, 1)
    counts = jnp.minimum(counts, inside_total)
    counts = counts.at[device_total - 1].set(1)
    counts = counts.at[0].set(inside_total[0])
    return (firsts, seconds, counts, (grid_x, grid_y, grid_z, slot_total))


def draw_pair_list(key, part):
    firsts, seconds, counts, extents = pair_tables(key)
    stacked = jnp.stack([firsts, seconds], axis=1)
    return stacked.reshape(extents[0], extents[1], extents[2], 2, extents[3]).astype(jnp.int32)


def draw_pair_count(key, part):
    firsts, seconds, counts, extents = pair_tables(key)
    return counts.reshape(extents[0], extents[1], extents[2]).astype(jnp.int32)


def with_ends(values, own_key, smallest, high):
    spot = [jax.random.randint(jax.random.fold_in(own_key, axis), (), 0, length) for axis, length in enumerate(values.shape)]
    main_axis = values.shape.index(max(values.shape))
    next_to = spot[:main_axis] + [(spot[main_axis] + 1) % values.shape[main_axis]] + spot[main_axis + 1:]
    return values.at[tuple(spot)].set(smallest).at[tuple(next_to)].set(high)


def block_scale(rng, shape, pieces, least, high):
    def one(dim, blocks):
        heights = jax.random.uniform(jax.random.fold_in(jax.random.fold_in(rng, 6), dim), (blocks,), jnp.float32, least / len(pieces), high / len(pieces))
        return jnp.repeat(jnp.exp(heights), shape[dim] // blocks).reshape((-1,) + (1,) * (len(shape) - dim - 1))

    gain = one(*pieces[0])
    for cut in pieces[1:]:
        gain = gain * one(*cut)
    return gain


def noise(rng, shape, deviation, reach, pieces=(), kind=jnp.bfloat16):
    result = deviation * jax.random.normal(rng, shape, jnp.float32)
    if pieces:
        result = result * block_scale(rng, shape, pieces, -0.22, 0.18)
    return jnp.clip(result, -reach, reach).astype(kind)


def setup_inputs(seed: int = 0) -> dict:
    key_list = jax.random.split(jax.random.key(seed), 13)
    return {
        "positions": jnp.clip(1.0 * jax.random.uniform(key_list[0], (NX, NY, NZ, 3, ATOMS), jnp.float32) ** block_scale(key_list[0], (NX, NY, NZ, 3, ATOMS), ((0, 4), (1, 4), (2, 2)), -0.2, 0.2), 0.0, 1.0),
        "velocities": noise(key_list[1], (NX, NY, NZ, 3, ATOMS), 1.0, 6.0, ((0, 4), (1, 4), (2, 2)), jnp.float32),
        "charges": noise(key_list[2], (NX, NY, NZ, ATOMS), 0.5, 3.0, ((0, 4), (1, 4), (2, 2)), jnp.float32),
        "atom_types": with_ends(jax.random.randint(key_list[3], (NX, NY, NZ, ATOMS), 0, NTYPES), jax.random.fold_in(key_list[3], 1), 0, NTYPES - 1).astype(jnp.int32),
        "atom_count": with_ends(jax.random.randint(key_list[4], (NX, NY, NZ), ATOMS // 4, ATOMS + 1), jax.random.fold_in(key_list[4], 1), ATOMS // 4, ATOMS).astype(jnp.int32),
        "sigma_type": jnp.clip(jnp.exp(jax.random.uniform(key_list[5], (NTYPES,), jnp.float32, math.log(0.15), math.log(0.35))), 0.15, 0.35),
        "epsilon_type": jnp.clip(jnp.exp(jax.random.uniform(key_list[6], (NTYPES,), jnp.float32, math.log(0.3), math.log(3.0))), 0.3, 3.0),
        "masses": jnp.clip(jnp.exp(math.log(4.0) - 1.3862944 * jax.random.uniform(key_list[7], (NX, NY, NZ, ATOMS), jnp.float32) ** block_scale(key_list[7], (NX, NY, NZ, ATOMS), ((0, 4), (1, 4), (2, 2)), -0.2, 0.2)), 1.0, 4.0),
        "pair_list": draw_pair_list(jax.random.fold_in(key_list[12], 71), 0),
        "pair_count": draw_pair_count(jax.random.fold_in(key_list[12], 71), 0),
        "pos_cotangent": noise(key_list[10], (NX, NY, NZ, 3, ATOMS), 1.0, 6.0, ((0, 4), (1, 4), (2, 2)), jnp.float32),
        "vel_cotangent": noise(key_list[11], (NX, NY, NZ, 3, ATOMS), 1.0, 6.0, ((0, 4), (1, 4), (2, 2)), jnp.float32),
    }


SOFT = 0.04
KAPPA = 2.0
COULOMB = 4.0
TIME_STEP = 0.004

def tile_energy(left_pos, right_pos, left_charge, right_charge, left_sigma, right_sigma, left_depth, right_depth, offset, same_block):
    separation = left_pos[:, :, None] - right_pos[:, None, :] + offset[:, None, None]
    distance = lax.optimization_barrier(jnp.sum(separation * separation, axis=0))
    mean_sigma = 0.5 * (left_sigma[:, None] + right_sigma[None, :])
    squared_sigma = mean_sigma * mean_sigma
    fraction = squared_sigma / (distance + squared_sigma)
    third_power = fraction * fraction * fraction
    dispersion = 4.0 * left_depth[:, None] * right_depth[None, :] * (third_power * third_power - third_power)
    radius = jnp.sqrt(distance + SOFT)
    screened = COULOMB * left_charge[:, None] * right_charge[None, :] * jnp.exp(-KAPPA * radius) / radius
    fading = jnp.maximum(1.0 - distance, 0.0)
    switch = fading * fading * fading
    per_block = left_pos.shape[1]
    diagonal = (lax.broadcasted_iota(jnp.int32, (per_block, per_block), 0) == lax.broadcasted_iota(jnp.int32, (per_block, per_block), 1)).astype(jnp.float32)
    weight = 1.0 - same_block * (0.5 + 0.5 * diagonal)
    return jnp.sum(weight * switch * (dispersion + screened))

def tile_forces(left_pos, right_pos, left_charge, right_charge, left_sigma, right_sigma, left_depth, right_depth, offset, same_block):
    gradients = jax.grad(tile_energy, argnums=(0, 1))(left_pos, right_pos, left_charge, right_charge, left_sigma, right_sigma, left_depth, right_depth, offset, same_block)
    return (-gradients[0], -gradients[1])

def pair_terms(flat_pos, flat_par, flat_cot, first_ids, second_ids, offset, same_block, live_slot, with_forces):
    left_pos = jnp.take(flat_pos, first_ids, axis=0)
    right_pos = jnp.take(flat_pos, second_ids, axis=0)
    left_par = jnp.take(flat_par, first_ids, axis=0)
    right_par = jnp.take(flat_par, second_ids, axis=0)
    slot_mask = live_slot[:, None, None]

    def batch_forces(pos_one, pos_two, charge_one, charge_two):
        return jax.vmap(tile_forces)(pos_one, pos_two, charge_one, charge_two, left_par[:, 1], right_par[:, 1], left_par[:, 2], right_par[:, 2], offset, same_block)
    if flat_cot is None:
        left_force, right_force = batch_forces(left_pos, right_pos, left_par[:, 0], right_par[:, 0])
        return (left_force * slot_mask, right_force * slot_mask)
    results, pullback = jax.vjp(batch_forces, left_pos, right_pos, left_par[:, 0], right_par[:, 0])
    left_cot = jnp.take(flat_cot, first_ids, axis=0) * slot_mask
    right_cot = jnp.take(flat_cot, second_ids, axis=0) * slot_mask
    pulled = pullback((left_cot, right_cot))
    left_rows = [pulled[0], pulled[2][:, None, :]]
    right_rows = [pulled[1], pulled[3][:, None, :]]
    if with_forces:
        left_rows = [results[0] * slot_mask] + left_rows
        right_rows = [results[1] * slot_mask] + right_rows
    return (jnp.concatenate(left_rows, axis=1), jnp.concatenate(right_rows, axis=1))

def atom_params(charges, atom_types, atom_count, sigma_type, epsilon_type):
    type_total = sigma_type.shape[0]
    alive_mask = (lax.broadcasted_iota(jnp.int32, charges.shape, charges.ndim - 1) < atom_count[..., None]).astype(jnp.float32)
    matches = (atom_types[..., None, :] == lax.broadcasted_iota(jnp.int32, (type_total, 1), 0)).astype(jnp.float32)
    sigma_atom = lax.optimization_barrier(jnp.sum(matches * sigma_type[:, None], axis=-2))
    depth_atom = lax.optimization_barrier(jnp.sum(matches * epsilon_type[:, None], axis=-2))
    params = jnp.stack([charges * alive_mask, sigma_atom, jnp.sqrt(depth_atom) * alive_mask], axis=-2)
    return (alive_mask, params)

def global_pairs(pair_list, pair_count):
    grid_x, grid_y, grid_z, unused, slot_total = pair_list.shape
    grid_shape = (grid_x, grid_y, grid_z, slot_total)

    def local_coords(index):
        return (index // ((BY + 1) * (BZ + 1)), index // (BZ + 1) % (BY + 1), index % (BZ + 1))
    anchor_x = lax.broadcasted_iota(jnp.int32, grid_shape, 0) * BX
    anchor_y = lax.broadcasted_iota(jnp.int32, grid_shape, 1) * BY
    anchor_z = lax.broadcasted_iota(jnp.int32, grid_shape, 2) * BZ
    left_local = local_coords(pair_list[:, :, :, 0, :])
    right_local = local_coords(pair_list[:, :, :, 1, :])

    def global_index(coords):
        return ((coords[0] + anchor_x) * NY + (coords[1] + anchor_y)) * NZ + (coords[2] + anchor_z)
    live_grid = lax.broadcasted_iota(jnp.int32, grid_shape, 3) < pair_count[..., None]
    zero_ids = jnp.zeros(grid_shape, jnp.int32)
    first_ids = jnp.where(live_grid, global_index(left_local).astype(jnp.int32), zero_ids).astype(jnp.int32).reshape(-1)
    second_ids = jnp.where(live_grid, global_index(right_local).astype(jnp.int32), zero_ids).astype(jnp.int32).reshape(-1)
    offsets = jnp.stack([(left_local[column] - right_local[column]).astype(jnp.float32) for column in range(3)], axis=-1).reshape(-1, 3)
    same_block = (pair_list[:, :, :, 0, :] == pair_list[:, :, :, 1, :]).astype(jnp.float32).reshape(-1)
    live_slot = live_grid.astype(jnp.float32).reshape(-1)
    return (first_ids, second_ids, offsets, same_block, live_slot)

def reference(positions, velocities, charges, atom_types, atom_count, sigma_type, epsilon_type, masses, pair_list, pair_count, pos_cotangent, vel_cotangent):
    alive_mask, params = atom_params(charges, atom_types, atom_count, sigma_type, epsilon_type)
    blocks_total = NX * NY * NZ
    per_block = positions.shape[-1]
    flat_par = params.reshape(blocks_total, 3, per_block)
    first_ids, second_ids, offsets, same_block, live_slot = global_pairs(pair_list, pair_count)
    group = pair_list.shape[-1]
    batches = (first_ids.reshape(-1, group), second_ids.reshape(-1, group), offsets.reshape(-1, group, 3), same_block.reshape(-1, group), live_slot.reshape(-1, group))

    def evaluate(flat_pos, flat_cot):
        rows_total = 3 if flat_cot is None else 4

        def one_batch(totals, batch):
            first_batch, second_batch, offset_batch, same_batch, slot_batch = batch
            left_rows, right_rows = pair_terms(flat_pos, flat_par, flat_cot, first_batch, second_batch, offset_batch, same_batch, slot_batch, False)
            totals = totals.at[first_batch].add(left_rows).at[second_batch].add(right_rows)
            return (totals, None)
        totals, unused = lax.scan(one_batch, jnp.zeros((blocks_total, rows_total, per_block), jnp.float32), batches)
        return totals
    inverse = (1.0 / masses).reshape(blocks_total, 1, per_block)
    half_step = 0.5 * TIME_STEP
    position = positions.reshape(blocks_total, 3, per_block)
    velocity = velocities.reshape(blocks_total, 3, per_block)
    history = [position]
    forces = evaluate(position, None)
    for step_index in range(STEPS):
        midway = velocity + half_step * inverse * forces
        position = position + TIME_STEP * midway
        history.append(position)
        forces = evaluate(position, None)
        velocity = midway + half_step * inverse * forces
    grad_position = pos_cotangent.reshape(blocks_total, 3, per_block)
    grad_velocity = vel_cotangent.reshape(blocks_total, 3, per_block)
    charge_sum = jnp.zeros((blocks_total, per_block), jnp.float32)
    pulled = evaluate(history[STEPS], half_step * inverse * grad_velocity)
    grad_position = grad_position + pulled[:, :3]
    charge_sum = charge_sum + pulled[:, 3]
    for step_index in range(STEPS - 1, -1, -1):
        grad_velocity = grad_velocity + TIME_STEP * grad_position
        factor = TIME_STEP if step_index > 0 else half_step
        pulled = evaluate(history[step_index], factor * inverse * grad_velocity)
        grad_position = grad_position + pulled[:, :3]
        charge_sum = charge_sum + pulled[:, 3]
    grad_charge = charge_sum * alive_mask.reshape(blocks_total, per_block)
    vector_shape = (NX, NY, NZ, 3, per_block)
    return (position.reshape(vector_shape), velocity.reshape(vector_shape), grad_position.reshape(vector_shape), grad_velocity.reshape(vector_shape), grad_charge.reshape(NX, NY, NZ, per_block))
```

```python
import functools

import jax
import jax.numpy as jnp
from jax import lax
from jax.experimental import pallas as pl
from jax.experimental.pallas import tpu as pltpu
from jax.sharding import PartitionSpec as P

STEPS = 5


SOFT = 0.04
KAPPA = 2.0
TIME_STEP = 0.004
CHUNK = 32


def passed_along(value, axis, steps):
    count = lax.axis_size(axis)
    leading, last = (max(0, -steps), min(count, count - steps))
    return lax.ppermute(value, axis, [(source, source + steps) for source in range(leading, last)])


def atom_params(charges, atom_types, atom_count, sigma_type, epsilon_type):
    type_total = sigma_type.shape[0]
    alive_mask = (
        lax.broadcasted_iota(jnp.int32, charges.shape, charges.ndim - 1) < atom_count[..., None]
    ).astype(jnp.float32)
    matches = (
        atom_types[..., None, :] == lax.broadcasted_iota(jnp.int32, (type_total, 1), 0)
    ).astype(jnp.float32)
    sigma_atom = jnp.sum(matches * sigma_type[:, None], axis=-2)
    depth_atom = jnp.sum(matches * epsilon_type[:, None], axis=-2)
    params = jnp.stack(
        [charges * alive_mask, 0.5 * sigma_atom, jnp.sqrt(depth_atom) * alive_mask, alive_mask],
        axis=-2,
    )
    return (alive_mask, params)


def rim_import(field):
    upper = passed_along(field, "gx", -1)
    field = jnp.concatenate([field, upper], axis=0)
    upper = passed_along(field[:, :1], "gy", -1)
    field = jnp.concatenate([field, upper], axis=1)
    upper = passed_along(field, "gz", -1)
    return jnp.concatenate([field, upper], axis=2)


def rim_return(field):
    lower = passed_along(field[:, :, -1:], "gz", 1)
    field = jnp.concatenate([field[:, :, :1] + lower, field[:, :, 1:-1]], axis=2)
    lower = passed_along(field[:, -1:], "gy", 1)
    field = jnp.concatenate([field[:, :1] + lower, field[:, 1:-1]], axis=1)
    lower = passed_along(field[-1:], "gx", 1)
    return jnp.concatenate([field[:1] + lower, field[1:-1]], axis=0)


def sweep_kernel(extent, force, adjoint, *refs):
    refs = list(refs)
    pair_ref, live_ref, size_ref, pos_ref, par_ref = refs[:5]
    refs = refs[5:]
    cot_ref = refs.pop(0) if adjoint else None
    out_ref, state_ref, column_ref, row_ref, lane_ref = refs
    total, unused, per_block = pos_ref.shape
    extent_y, extent_z = extent
    rows_out = out_ref.shape[1]
    full = (8, per_block)

    def prepare(block, carry):
        state_ref[block, 0:3, :] = pos_ref[block]
        state_ref[block, 3:7, :] = par_ref[block]
        if adjoint:
            state_ref[block, 8:11, :] = cot_ref[block]
        column_ref[block] = state_ref[block].T
        for part in range(rows_out):
            row_ref[block, part] = jnp.zeros((per_block, per_block), jnp.float32)
            lane_ref[block, part] = jnp.zeros(full, jnp.float32)
        return carry

    lax.fori_loop(0, total, prepare, 0)

    def coords(index):
        return (index // (extent_y * extent_z), index // extent_z % extent_y, index % extent_z)

    def one_pair(slot, carry):
        first = pair_ref[0, slot]
        second = pair_ref[1, slot]
        swap = size_ref[first] > size_ref[second]
        rows = jnp.where(swap, second, first)
        lanes = jnp.where(swap, first, second)
        weight = jnp.where(first == second, 0.5, 1.0).astype(jnp.float32)
        row_coords = coords(rows)
        lane_coords = coords(lanes)

        def lane_row(part):
            return jnp.broadcast_to(state_ref[lanes, part : part + 1, :], full)

        lane_pos = [
            lane_row(axis) - (row_coords[axis] - lane_coords[axis]).astype(jnp.float32)
            for axis in range(3)
        ]
        lane_charge = lane_row(3) * (8.0 * weight)
        lane_sigma = lane_row(4)
        lane_depth = lane_row(5) * (24.0 * weight)
        lane_cot = [lane_row(8 + axis) for axis in range(3)] if adjoint else None

        def one_chunk(chunk, sums):
            sums = list(sums)
            for group in range(CHUNK // 8):
                start = pl.multiple_of(chunk * CHUNK + group * 8, 8)
                columns = column_ref[rows, pl.ds(start, 8), :]

                def row_column(part):
                    return jnp.broadcast_to(columns[:, part : part + 1], full)

                d = [row_column(axis) - lane_pos[axis] for axis in range(3)]
                s = d[0] * d[0] + d[1] * d[1] + d[2] * d[2]
                sigma = row_column(4) + lane_sigma
                square = sigma * sigma
                inverse = 1.0 / (s + square)
                t = square * inverse
                t3 = t * t * t
                soft = s + SOFT
                r = lax.rsqrt(soft)
                b = jnp.exp(-KAPPA * (soft * r)) * r
                c = jnp.maximum(1.0 - s, 0.0)
                cc = c * c
                p = c * inverse
                y = c * r
                row_charge = row_column(3)
                et = row_column(5) * lane_depth * t3
                below = t3 - 1.0
                twice = t3 + below
                half = 1.0 + 0.5 * r
                k1 = 3.0 + y * half
                charge_b = lane_charge * b
                qb = row_charge * charge_b
                g1 = cc * (et * (below + p * twice) + qb * k1)
                results = []
                if force:
                    results += [g1 * d[axis] for axis in range(3)]
                if adjoint:
                    h = p * (p * (7.0 * t3 - 2.0) + 3.0 * twice) + below
                    k2 = y * (y * (1.0 + r * (1.5 + 0.75 * r)) + 6.0 * half) + 6.0
                    k = -2.0 * c * (2.0 * et * h + qb * k2)
                    delta = [row_column(8 + axis) - lane_cot[axis] for axis in range(3)]
                    along = delta[0] * d[0] + delta[1] * d[1] + delta[2] * d[2]
                    ka = k * along
                    results += [g1 * delta[axis] + ka * d[axis] for axis in range(3)]
                    m = cc * k1 * along
                for part, value in enumerate(results):
                    row_ref[rows, part, pl.ds(start, 8), :] += value
                    sums[part] = sums[part] + value
                if adjoint:
                    last = rows_out - 1
                    row_ref[rows, last, pl.ds(start, 8), :] += m * charge_b
                    sums[last] = sums[last] + (m * b) * row_charge
            return tuple(sums)

        chunks = (size_ref[rows] + CHUNK - 1) // CHUNK
        zero = jnp.zeros(full, jnp.float32)
        sums = lax.fori_loop(0, chunks, one_chunk, (zero,) * rows_out)
        vectors = rows_out - 1 if adjoint else rows_out
        for part in range(vectors):
            lane_ref[lanes, part] -= sums[part]
        if adjoint:
            lane_ref[lanes, vectors] += sums[vectors] * (8.0 * weight)
        return carry

    lax.fori_loop(0, live_ref[0], one_pair, 0)

    which = lax.broadcasted_iota(jnp.int32, (per_block, 8), 1)

    def finish(block, carry):
        columns = jnp.zeros((per_block, 8), jnp.float32)
        for part in range(rows_out):
            summed = jnp.sum(row_ref[block, part], axis=1, keepdims=True)
            columns = jnp.where(which == part, summed, columns)
        turned = columns.T
        for part in range(rows_out):
            out_ref[block, part : part + 1, :] = turned[part : part + 1, :] + jnp.sum(
                lane_ref[block, part], axis=0, keepdims=True
            )
        return carry

    lax.fori_loop(0, total, finish, 0)


def sweep(ext_pos, ext_par, sizes, pair_list, pair_count, ext_cot, force):
    extent = ext_pos.shape[:3]
    per_block = ext_pos.shape[-1]
    total = extent[0] * extent[1] * extent[2]
    adjoint = ext_cot is not None
    rows_out = (3 if force else 0) + (4 if adjoint else 0)
    operands = [
        pair_list[0, 0, 0],
        pair_count.reshape(1),
        sizes,
        ext_pos.reshape(total, 3, per_block),
        ext_par,
    ]
    if adjoint:
        operands.append(ext_cot.reshape(total, 3, per_block))
    smem = pl.BlockSpec(memory_space=pltpu.SMEM)
    vmem = pl.BlockSpec(memory_space=pltpu.VMEM)
    height = 16 if adjoint else 8
    out = pl.pallas_call(
        functools.partial(sweep_kernel, extent[1:], force, adjoint),
        out_shape=jax.ShapeDtypeStruct((total, rows_out, per_block), jnp.float32),
        in_specs=[smem] * 3 + [vmem] * (len(operands) - 3),
        out_specs=vmem,
        scratch_shapes=[
            pltpu.VMEM((total, height, per_block), jnp.float32),
            pltpu.VMEM((total, per_block, height), jnp.float32),
            pltpu.VMEM((total, rows_out, per_block, per_block), jnp.float32),
            pltpu.VMEM((total, rows_out, 8, per_block), jnp.float32),
        ],
        compiler_params=pltpu.CompilerParams(vmem_limit_bytes=40 * 1024 * 1024),
    )(*operands)
    return out.reshape(extent + (rows_out, per_block))


def on_device(
    positions,
    velocities,
    charges,
    atom_types,
    atom_count,
    sigma_type,
    epsilon_type,
    masses,
    pair_list,
    pair_count,
    pos_cotangent,
    vel_cotangent,
):
    alive_mask, params = atom_params(charges, atom_types, atom_count, sigma_type, epsilon_type)
    inverse = (1.0 / masses)[..., None, :]
    half_step = 0.5 * TIME_STEP
    extended = rim_import(jnp.concatenate([positions, params], axis=3))
    ext_pos = extended[:, :, :, :3]
    per_block = positions.shape[-1]
    ext_par = extended[:, :, :, 3:].reshape(-1, 4, per_block)
    sizes = jnp.sum(ext_par[:, 3], axis=-1).astype(jnp.int32)
    history = [ext_pos]
    position = positions
    velocity = velocities
    grad_position = pos_cotangent
    grad_velocity = vel_cotangent
    for step_index in range(STEPS):
        forces = rim_return(
            sweep(history[-1], ext_par, sizes, pair_list, pair_count, None, True)
        )
        factor = half_step if step_index == 0 else TIME_STEP
        velocity = velocity + factor * inverse * forces
        position = position + TIME_STEP * velocity
        history.append(rim_import(position))
    last_cot = rim_import(half_step * inverse * grad_velocity)
    pulled = rim_return(
        sweep(history[STEPS], ext_par, sizes, pair_list, pair_count, last_cot, True)
    )
    velocity = velocity + half_step * inverse * pulled[:, :, :, :3]
    grad_position = grad_position + pulled[:, :, :, 3:6]
    charge_sum = pulled[:, :, :, 6]
    for step_index in range(STEPS - 1, -1, -1):
        grad_velocity = grad_velocity + TIME_STEP * grad_position
        factor = TIME_STEP if step_index > 0 else half_step
        ext_cot = rim_import(factor * inverse * grad_velocity)
        pulled = rim_return(
            sweep(history[step_index], ext_par, sizes, pair_list, pair_count, ext_cot, False)
        )
        grad_position = grad_position + pulled[:, :, :, :3]
        charge_sum = charge_sum + pulled[:, :, :, 3]
    return (position, velocity, grad_position, grad_velocity, charge_sum * alive_mask)


def solution(mesh):
    in_specs = (
        P("gx", "gy", "gz", None, None),
        P("gx", "gy", "gz", None, None),
        P("gx", "gy", "gz", None),
        P("gx", "gy", "gz", None),
        P("gx", "gy", "gz"),
        P(),
        P(),
        P("gx", "gy", "gz", None),
        P("gx", "gy", "gz", None, None),
        P("gx", "gy", "gz"),
        P("gx", "gy", "gz", None, None),
        P("gx", "gy", "gz", None, None),
    )
    out_specs = (
        P("gx", "gy", "gz", None, None),
        P("gx", "gy", "gz", None, None),
        P("gx", "gy", "gz", None, None),
        P("gx", "gy", "gz", None, None),
        P("gx", "gy", "gz", None),
    )
    return jax.shard_map(
        on_device, mesh=mesh, in_specs=in_specs, out_specs=out_specs, check_vma=False
    )
```

```python
import functools

import jax
import jax.numpy as jnp
from jax import lax
from jax.experimental import pallas as pl
from jax.experimental.pallas import tpu as pltpu
from jax.sharding import PartitionSpec as P

STEPS = 5


SOFT = 0.04
KAPPA = 2.0
TIME_STEP = 0.004
CHUNK = 32


def atom_params(charges, atom_types, atom_count, sigma_type, epsilon_type):
    type_total = sigma_type.shape[0]
    alive_mask = (
        lax.broadcasted_iota(jnp.int32, charges.shape, charges.ndim - 1) < atom_count[..., None]
    ).astype(jnp.float32)
    matches = (
        atom_types[..., None, :] == lax.broadcasted_iota(jnp.int32, (type_total, 1), 0)
    ).astype(jnp.float32)
    sigma_atom = jnp.sum(matches * sigma_type[:, None], axis=-2)
    depth_atom = jnp.sum(matches * epsilon_type[:, None], axis=-2)
    params = jnp.stack(
        [charges * alive_mask, 0.5 * sigma_atom, jnp.sqrt(depth_atom) * alive_mask, alive_mask],
        axis=-2,
    )
    return (alive_mask, params)


AXES = ("gx", "gy", "gz")
SIDES = [(x, y, z) for x in (0, 1) for y in (0, 1) for z in (0, 1)][1:]


def low_part(side, own):
    return tuple(pl.ds(0, 1 if d else n) for d, n in zip(side, own))


def rim_part(side, own):
    return tuple(pl.ds(n, 1) if d else pl.ds(0, n) for d, n in zip(side, own))


class Neighbours:
    def __init__(self, counts):
        self.counts = counts
        self.here = tuple(lax.axis_index(axis) for axis in AXES)

    def at(self, side, sign):
        return tuple(place + sign * step for place, step in zip(self.here, side))

    def exists(self, side, sign):
        found = None
        for place, step, count in zip(self.here, side, self.counts):
            if step:
                test = place < count - 1 if sign > 0 else place > 0
                found = test if found is None else jnp.logical_and(found, test)
        return found

    def greet(self):
        barrier = pltpu.get_barrier_semaphore()
        for sign in (1, -1):
            for side in SIDES:

                @pl.when(self.exists(side, sign))
                def _(side=side, sign=sign):
                    pl.semaphore_signal(
                        barrier,
                        inc=1,
                        device_id=self.at(side, sign),
                        device_id_type=pl.DeviceIdType.MESH,
                    )

        peers = sum(
            self.exists(side, sign).astype(jnp.int32) for sign in (1, -1) for side in SIDES
        )
        pl.semaphore_wait(barrier, peers)

    def copy(self, source, target, sems, index, side, sign):
        return pltpu.make_async_remote_copy(
            src_ref=source,
            dst_ref=target,
            send_sem=sems.at[0, index],
            recv_sem=sems.at[1, index],
            device_id=self.at(side, sign),
            device_id_type=pl.DeviceIdType.MESH,
        )


def returned_sum(near, part_ref, total_ref, landing, sems, own):
    def moved(index, side):
        return near.copy(
            part_ref.at[rim_part(side, own)], landing[index], sems, index, side, 1
        )

    for index, side in enumerate(SIDES):

        @pl.when(near.exists(side, 1))
        def _(index=index, side=side):
            moved(index, side).start()

    total_ref[...] = part_ref[tuple(pl.ds(0, n) for n in own)]
    for index, side in enumerate(SIDES):

        @pl.when(near.exists(side, -1))
        def _(index=index, side=side):
            moved(index, side).wait_recv()
            where = low_part(side, own)
            total_ref[where] = total_ref[where] + landing[index][...]

    def finish():
        for index, side in enumerate(SIDES):

            @pl.when(near.exists(side, 1))
            def _(index=index, side=side):
                moved(index, side).wait_send()

    return finish


def spread(near, value, ext_ref, sems, own):
    ext_ref[tuple(pl.ds(0, n) for n in own)] = value
    base = len(SIDES)

    def moved(index, side):
        return near.copy(
            ext_ref.at[low_part(side, own)],
            ext_ref.at[rim_part(side, own)],
            sems,
            base + index,
            side,
            -1,
        )

    for index, side in enumerate(SIDES):

        @pl.when(near.exists(side, -1))
        def _(index=index, side=side):
            moved(index, side).start()

    for index, side in enumerate(SIDES):

        @pl.when(jnp.logical_not(near.exists(side, 1)))
        def _(index=index, side=side):
            where = rim_part(side, own)
            shape = tuple(1 if d else n for d, n in zip(side, own)) + ext_ref.shape[3:]
            ext_ref[where] = jnp.zeros(shape, jnp.float32)

    def finish():
        for index, side in enumerate(SIDES):

            @pl.when(near.exists(side, 1))
            def _(index=index, side=side):
                moved(index, side).wait_recv()

        for index, side in enumerate(SIDES):

            @pl.when(near.exists(side, -1))
            def _(index=index, side=side):
                moved(index, side).wait_send()

    return finish


def first_kernel(counts, own, field_ref, ext_ref, sems):
    near = Neighbours(counts)
    near.greet()
    spread(near, field_ref[...], ext_ref, sems, own)()


def forward_kernel(counts, own, part, ext_old, vel, scale, ext_ref, vel_out, total, *rest):
    landing, sems = rest[:-1], rest[-1]
    near = Neighbours(counts)
    near.greet()
    sent = returned_sum(near, part, total, landing, sems, own)
    velocity = vel[...] + scale[...] * total[...]
    vel_out[...] = velocity
    position = ext_old[tuple(pl.ds(0, n) for n in own)] + TIME_STEP * velocity
    spread(near, position, ext_ref, sems, own)()
    sent()


def turn_kernel(
    counts, own, part, vel, vel_scale, gpos, gvel, scale,
    ext_ref, gpos_out, gvel_out, charge_out, vel_out, total, *rest,
):
    landing, sems = rest[:-1], rest[-1]
    near = Neighbours(counts)
    near.greet()
    sent = returned_sum(near, part, total, landing, sems, own)
    grad_position = gpos[...] + total[:, :, :, 3:6, :]
    grad_velocity = gvel[...] + TIME_STEP * grad_position
    finish = spread(near, scale[...] * grad_velocity, ext_ref, sems, own)
    gpos_out[...] = grad_position
    gvel_out[...] = grad_velocity
    charge_out[...] = total[:, :, :, 6:7, :]
    vel_out[...] = vel[...] + vel_scale[...] * total[:, :, :, 0:3, :]
    finish()
    sent()


def backward_kernel(
    counts, own, part, gpos, gvel, scale, charge,
    ext_ref, gpos_out, gvel_out, charge_out, total, *rest,
):
    landing, sems = rest[:-1], rest[-1]
    near = Neighbours(counts)
    near.greet()
    sent = returned_sum(near, part, total, landing, sems, own)
    grad_position = gpos[...] + total[:, :, :, 0:3, :]
    grad_velocity = gvel[...] + TIME_STEP * grad_position
    finish = spread(near, scale[...] * grad_velocity, ext_ref, sems, own)
    gpos_out[...] = grad_position
    gvel_out[...] = grad_velocity
    charge_out[...] = charge[...] + total[:, :, :, 3:4, :]
    finish()
    sent()


def last_kernel(counts, own, part, gpos, charge, alive, gpos_out, charge_out, total, *rest):
    landing, sems = rest[:-1], rest[-1]
    near = Neighbours(counts)
    near.greet()
    sent = returned_sum(near, part, total, landing, sems, own)
    gpos_out[...] = gpos[...] + total[:, :, :, 0:3, :]
    charge_out[...] = (charge[...] + total[:, :, :, 3:4, :]) * alive[...]
    sent()


def exchange(kernel, identity, own, rows_in, rows_out, *operands):
    counts = tuple(lax.axis_size(axis) for axis in AXES)
    per_block = operands[0].shape[-1]
    extended = tuple(n + 1 for n in own)
    outs = [
        jax.ShapeDtypeStruct((extended if rim else own) + (rows, per_block), jnp.float32)
        for rim, rows in rows_out
    ]
    scratch = []
    if rows_in:
        scratch.append(pltpu.VMEM(own + (rows_in, per_block), jnp.float32))
        for side in SIDES:
            shape = tuple(1 if d else n for d, n in zip(side, own))
            scratch.append(pltpu.VMEM(shape + (rows_in, per_block), jnp.float32))
    scratch.append(pltpu.SemaphoreType.DMA((2, 2 * len(SIDES))))
    vmem = pl.BlockSpec(memory_space=pltpu.VMEM)
    return pl.pallas_call(
        functools.partial(kernel, counts, own),
        out_shape=outs,
        in_specs=[vmem] * len(operands),
        out_specs=[vmem] * len(outs),
        scratch_shapes=scratch,
        compiler_params=pltpu.CompilerParams(
            collective_id=identity, has_side_effects=True, vmem_limit_bytes=4 * 1024 * 1024
        ),
    )(*operands)


def sweep_kernel(extent, force, adjoint, *refs):
    refs = list(refs)
    pair_ref, live_ref, size_ref, pos_ref, par_ref = refs[:5]
    refs = refs[5:]
    cot_ref = refs.pop(0) if adjoint else None
    out_ref, state_ref, column_ref, row_ref, lane_ref = refs
    total, unused, per_block = pos_ref.shape
    extent_y, extent_z = extent
    rows_out = out_ref.shape[1]
    full = (8, per_block)

    def prepare(block, carry):
        state_ref[block, 0:3, :] = pos_ref[block]
        state_ref[block, 3:7, :] = par_ref[block]
        if adjoint:
            state_ref[block, 8:11, :] = cot_ref[block]
        column_ref[block] = state_ref[block].T
        for part in range(rows_out):
            row_ref[block, part] = jnp.zeros((per_block, per_block), jnp.float32)
            lane_ref[block, part] = jnp.zeros(full, jnp.float32)
        return carry

    lax.fori_loop(0, total, prepare, 0)

    def coords(index):
        return (index // (extent_y * extent_z), index // extent_z % extent_y, index % extent_z)

    def one_pair(slot, carry):
        first = pair_ref[0, slot]
        second = pair_ref[1, slot]
        swap = size_ref[first] > size_ref[second]
        rows = jnp.where(swap, second, first)
        lanes = jnp.where(swap, first, second)
        weight = jnp.where(first == second, 0.5, 1.0).astype(jnp.float32)
        row_coords = coords(rows)
        lane_coords = coords(lanes)

        def lane_row(part):
            return jnp.broadcast_to(state_ref[lanes, part : part + 1, :], full)

        lane_pos = [
            lane_row(axis) - (row_coords[axis] - lane_coords[axis]).astype(jnp.float32)
            for axis in range(3)
        ]
        lane_charge = lane_row(3) * (8.0 * weight)
        lane_sigma = lane_row(4)
        lane_depth = lane_row(5) * (24.0 * weight)
        lane_cot = [lane_row(8 + axis) for axis in range(3)] if adjoint else None

        def one_chunk(chunk, sums):
            sums = list(sums)
            for group in range(CHUNK // 8):
                start = pl.multiple_of(chunk * CHUNK + group * 8, 8)
                columns = column_ref[rows, pl.ds(start, 8), :]

                def row_column(part):
                    return jnp.broadcast_to(columns[:, part : part + 1], full)

                d = [row_column(axis) - lane_pos[axis] for axis in range(3)]
                s = d[0] * d[0] + d[1] * d[1] + d[2] * d[2]
                sigma = row_column(4) + lane_sigma
                square = sigma * sigma
                inverse = 1.0 / (s + square)
                t = square * inverse
                t3 = t * t * t
                soft = s + SOFT
                r = lax.rsqrt(soft)
                b = jnp.exp(-KAPPA * (soft * r)) * r
                c = jnp.maximum(1.0 - s, 0.0)
                cc = c * c
                p = c * inverse
                y = c * r
                row_charge = row_column(3)
                et = row_column(5) * lane_depth * t3
                below = t3 - 1.0
                twice = t3 + below
                half = 1.0 + 0.5 * r
                k1 = 3.0 + y * half
                charge_b = lane_charge * b
                qb = row_charge * charge_b
                g1 = cc * (et * (below + p * twice) + qb * k1)
                results = []
                if force:
                    results += [g1 * d[axis] for axis in range(3)]
                if adjoint:
                    h = p * (p * (7.0 * t3 - 2.0) + 3.0 * twice) + below
                    k2 = y * (y * (1.0 + r * (1.5 + 0.75 * r)) + 6.0 * half) + 6.0
                    k = -2.0 * c * (2.0 * et * h + qb * k2)
                    delta = [row_column(8 + axis) - lane_cot[axis] for axis in range(3)]
                    along = delta[0] * d[0] + delta[1] * d[1] + delta[2] * d[2]
                    ka = k * along
                    results += [g1 * delta[axis] + ka * d[axis] for axis in range(3)]
                    m = cc * k1 * along
                for part, value in enumerate(results):
                    row_ref[rows, part, pl.ds(start, 8), :] += value
                    sums[part] = sums[part] + value
                if adjoint:
                    last = rows_out - 1
                    row_ref[rows, last, pl.ds(start, 8), :] += m * charge_b
                    sums[last] = sums[last] + (m * b) * row_charge
            return tuple(sums)

        chunks = (size_ref[rows] + CHUNK - 1) // CHUNK
        zero = jnp.zeros(full, jnp.float32)
        sums = lax.fori_loop(0, chunks, one_chunk, (zero,) * rows_out)
        vectors = rows_out - 1 if adjoint else rows_out
        for part in range(vectors):
            lane_ref[lanes, part] -= sums[part]
        if adjoint:
            lane_ref[lanes, vectors] += sums[vectors] * (8.0 * weight)
        return carry

    lax.fori_loop(0, live_ref[0], one_pair, 0)

    which = lax.broadcasted_iota(jnp.int32, (per_block, 8), 1)

    def finish(block, carry):
        columns = jnp.zeros((per_block, 8), jnp.float32)
        for part in range(rows_out):
            summed = jnp.sum(row_ref[block, part], axis=1, keepdims=True)
            columns = jnp.where(which == part, summed, columns)
        turned = columns.T
        for part in range(rows_out):
            out_ref[block, part : part + 1, :] = turned[part : part + 1, :] + jnp.sum(
                lane_ref[block, part], axis=0, keepdims=True
            )
        return carry

    lax.fori_loop(0, total, finish, 0)


def sweep(ext_pos, ext_par, sizes, pair_list, pair_count, ext_cot, force):
    extent = ext_pos.shape[:3]
    per_block = ext_pos.shape[-1]
    total = extent[0] * extent[1] * extent[2]
    adjoint = ext_cot is not None
    rows_out = (3 if force else 0) + (4 if adjoint else 0)
    operands = [
        pair_list[0, 0, 0],
        pair_count.reshape(1),
        sizes,
        ext_pos.reshape(total, 3, per_block),
        ext_par,
    ]
    if adjoint:
        operands.append(ext_cot.reshape(total, 3, per_block))
    smem = pl.BlockSpec(memory_space=pltpu.SMEM)
    vmem = pl.BlockSpec(memory_space=pltpu.VMEM)
    height = 16 if adjoint else 8
    out = pl.pallas_call(
        functools.partial(sweep_kernel, extent[1:], force, adjoint),
        out_shape=jax.ShapeDtypeStruct((total, rows_out, per_block), jnp.float32),
        in_specs=[smem] * 3 + [vmem] * (len(operands) - 3),
        out_specs=vmem,
        scratch_shapes=[
            pltpu.VMEM((total, height, per_block), jnp.float32),
            pltpu.VMEM((total, per_block, height), jnp.float32),
            pltpu.VMEM((total, rows_out, per_block, per_block), jnp.float32),
            pltpu.VMEM((total, rows_out, 8, per_block), jnp.float32),
        ],
        compiler_params=pltpu.CompilerParams(vmem_limit_bytes=40 * 1024 * 1024),
    )(*operands)
    return out.reshape(extent + (rows_out, per_block))


def on_device(
    positions,
    velocities,
    charges,
    atom_types,
    atom_count,
    sigma_type,
    epsilon_type,
    masses,
    pair_list,
    pair_count,
    pos_cotangent,
    vel_cotangent,
):
    alive_mask, params = atom_params(charges, atom_types, atom_count, sigma_type, epsilon_type)
    inverse = (1.0 / masses)[..., None, :]
    half_step = 0.5 * TIME_STEP
    own = positions.shape[:3]
    per_block = positions.shape[-1]
    half_scale = jnp.broadcast_to(half_step * inverse, positions.shape)
    full_scale = jnp.broadcast_to(TIME_STEP * inverse, positions.shape)
    field = jnp.concatenate([positions, params, half_scale * vel_cotangent], axis=3)
    (extended,) = exchange(first_kernel, 1, own, 0, [(True, 10)], field)
    ext_par = extended[:, :, :, 3:7].reshape(-1, 4, per_block)
    last_cot = extended[:, :, :, 7:10]
    sizes = jnp.sum(ext_par[:, 3], axis=-1).astype(jnp.int32)
    history = [extended[:, :, :, :3]]
    velocity = velocities
    for step_index in range(STEPS):
        part = sweep(history[-1], ext_par, sizes, pair_list, pair_count, None, True)
        scale = half_scale if step_index == 0 else full_scale
        ext_next, velocity = exchange(
            forward_kernel, 2, own, 3, [(True, 3), (False, 3)], part, history[-1], velocity, scale
        )
        history.append(ext_next)
    part = sweep(history[STEPS], ext_par, sizes, pair_list, pair_count, last_cot, True)
    ext_cot, grad_position, grad_velocity, charge_sum, velocity = exchange(
        turn_kernel,
        3,
        own,
        7,
        [(True, 3), (False, 3), (False, 3), (False, 1), (False, 3)],
        part,
        velocity,
        half_scale,
        pos_cotangent,
        vel_cotangent,
        full_scale,
    )
    for step_index in range(STEPS - 1, 0, -1):
        part = sweep(history[step_index], ext_par, sizes, pair_list, pair_count, ext_cot, False)
        scale = full_scale if step_index > 1 else half_scale
        ext_cot, grad_position, grad_velocity, charge_sum = exchange(
            backward_kernel,
            4,
            own,
            4,
            [(True, 3), (False, 3), (False, 3), (False, 1)],
            part,
            grad_position,
            grad_velocity,
            scale,
            charge_sum,
        )
    part = sweep(history[0], ext_par, sizes, pair_list, pair_count, ext_cot, False)
    grad_position, charge_sum = exchange(
        last_kernel,
        5,
        own,
        4,
        [(False, 3), (False, 1)],
        part,
        grad_position,
        charge_sum,
        alive_mask[..., None, :],
    )
    position = history[STEPS][: own[0], : own[1], : own[2]]
    return (position, velocity, grad_position, grad_velocity, charge_sum[:, :, :, 0])


def solution(mesh):
    in_specs = (
        P("gx", "gy", "gz", None, None),
        P("gx", "gy", "gz", None, None),
        P("gx", "gy", "gz", None),
        P("gx", "gy", "gz", None),
        P("gx", "gy", "gz"),
        P(),
        P(),
        P("gx", "gy", "gz", None),
        P("gx", "gy", "gz", None, None),
        P("gx", "gy", "gz"),
        P("gx", "gy", "gz", None, None),
        P("gx", "gy", "gz", None, None),
    )
    out_specs = (
        P("gx", "gy", "gz", None, None),
        P("gx", "gy", "gz", None, None),
        P("gx", "gy", "gz", None, None),
        P("gx", "gy", "gz", None, None),
        P("gx", "gy", "gz", None),
    )
    return jax.shard_map(
        on_device, mesh=mesh, in_specs=in_specs, out_specs=out_specs, check_vma=False
    )
```

```python
import functools

import jax
import jax.numpy as jnp
from jax import lax
from jax.experimental import pallas as pl
from jax.experimental.pallas import tpu as pltpu
from jax.sharding import PartitionSpec as P

STEPS = 5


SOFT = 0.04
KAPPA = 2.0
TIME_STEP = 0.004
CHUNK = 32
BATCH = 2


def atom_params(charges, atom_types, atom_count, sigma_type, epsilon_type):
    type_total = sigma_type.shape[0]
    alive_mask = (
        lax.broadcasted_iota(jnp.int32, charges.shape, charges.ndim - 1) < atom_count[..., None]
    ).astype(jnp.float32)
    matches = (
        atom_types[..., None, :] == lax.broadcasted_iota(jnp.int32, (type_total, 1), 0)
    ).astype(jnp.float32)
    sigma_atom = jnp.sum(matches * sigma_type[:, None], axis=-2)
    depth_atom = jnp.sum(matches * epsilon_type[:, None], axis=-2)
    params = jnp.stack(
        [charges * alive_mask, 0.5 * sigma_atom, jnp.sqrt(depth_atom) * alive_mask, alive_mask],
        axis=-2,
    )
    return (alive_mask, params)


AXES = ("gx", "gy", "gz")
SIDES = [(x, y, z) for x in (0, 1) for y in (0, 1) for z in (0, 1)][1:]


def low_part(side, own):
    return tuple(pl.ds(0, 1 if d else n) for d, n in zip(side, own))


def rim_part(side, own):
    return tuple(pl.ds(n, 1) if d else pl.ds(0, n) for d, n in zip(side, own))


class Neighbours:
    def __init__(self, counts):
        self.counts = counts
        self.here = tuple(lax.axis_index(axis) for axis in AXES)

    def at(self, side, sign):
        return tuple(place + sign * step for place, step in zip(self.here, side))

    def exists(self, side, sign):
        found = None
        for place, step, count in zip(self.here, side, self.counts):
            if step:
                test = place < count - 1 if sign > 0 else place > 0
                found = test if found is None else jnp.logical_and(found, test)
        return found

    def greet(self):
        barrier = pltpu.get_barrier_semaphore()
        for sign in (1, -1):
            for side in SIDES:

                @pl.when(self.exists(side, sign))
                def _(side=side, sign=sign):
                    pl.semaphore_signal(
                        barrier,
                        inc=1,
                        device_id=self.at(side, sign),
                        device_id_type=pl.DeviceIdType.MESH,
                    )

        peers = sum(
            self.exists(side, sign).astype(jnp.int32) for sign in (1, -1) for side in SIDES
        )
        pl.semaphore_wait(barrier, peers)

    def copy(self, source, target, sems, index, side, sign):
        return pltpu.make_async_remote_copy(
            src_ref=source,
            dst_ref=target,
            send_sem=sems.at[0, index],
            recv_sem=sems.at[1, index],
            device_id=self.at(side, sign),
            device_id_type=pl.DeviceIdType.MESH,
        )


def returned_sum(near, part_ref, total_ref, landing, sems, own):
    def moved(index, side):
        return near.copy(
            part_ref.at[rim_part(side, own)], landing[index], sems, index, side, 1
        )

    for index, side in enumerate(SIDES):

        @pl.when(near.exists(side, 1))
        def _(index=index, side=side):
            moved(index, side).start()

    total_ref[...] = part_ref[tuple(pl.ds(0, n) for n in own)]
    for index, side in enumerate(SIDES):

        @pl.when(near.exists(side, -1))
        def _(index=index, side=side):
            moved(index, side).wait_recv()
            where = low_part(side, own)
            total_ref[where] = total_ref[where] + landing[index][...]

    def finish():
        for index, side in enumerate(SIDES):

            @pl.when(near.exists(side, 1))
            def _(index=index, side=side):
                moved(index, side).wait_send()

    return finish


def spread(near, value, ext_ref, sems, own):
    ext_ref[tuple(pl.ds(0, n) for n in own)] = value
    base = len(SIDES)

    def moved(index, side):
        return near.copy(
            ext_ref.at[low_part(side, own)],
            ext_ref.at[rim_part(side, own)],
            sems,
            base + index,
            side,
            -1,
        )

    for index, side in enumerate(SIDES):

        @pl.when(near.exists(side, -1))
        def _(index=index, side=side):
            moved(index, side).start()

    for index, side in enumerate(SIDES):

        @pl.when(jnp.logical_not(near.exists(side, 1)))
        def _(index=index, side=side):
            where = rim_part(side, own)
            shape = tuple(1 if d else n for d, n in zip(side, own)) + ext_ref.shape[3:]
            ext_ref[where] = jnp.zeros(shape, jnp.float32)

    def finish():
        for index, side in enumerate(SIDES):

            @pl.when(near.exists(side, 1))
            def _(index=index, side=side):
                moved(index, side).wait_recv()

        for index, side in enumerate(SIDES):

            @pl.when(near.exists(side, -1))
            def _(index=index, side=side):
                moved(index, side).wait_send()

    return finish


def first_kernel(counts, own, field_ref, ext_ref, sems):
    near = Neighbours(counts)
    near.greet()
    spread(near, field_ref[...], ext_ref, sems, own)()


def forward_kernel(counts, own, part, ext_old, vel, scale, ext_ref, vel_out, total, *rest):
    landing, sems = rest[:-1], rest[-1]
    near = Neighbours(counts)
    near.greet()
    sent = returned_sum(near, part, total, landing, sems, own)
    velocity = vel[...] + scale[...] * total[...]
    vel_out[...] = velocity
    position = ext_old[tuple(pl.ds(0, n) for n in own)] + TIME_STEP * velocity
    spread(near, position, ext_ref, sems, own)()
    sent()


def turn_kernel(
    counts, own, part, vel, vel_scale, gpos, gvel, scale,
    ext_ref, gpos_out, gvel_out, charge_out, vel_out, total, *rest,
):
    landing, sems = rest[:-1], rest[-1]
    near = Neighbours(counts)
    near.greet()
    sent = returned_sum(near, part, total, landing, sems, own)
    grad_position = gpos[...] + total[:, :, :, 3:6, :]
    grad_velocity = gvel[...] + TIME_STEP * grad_position
    finish = spread(near, scale[...] * grad_velocity, ext_ref, sems, own)
    gpos_out[...] = grad_position
    gvel_out[...] = grad_velocity
    charge_out[...] = total[:, :, :, 6:7, :]
    vel_out[...] = vel[...] + vel_scale[...] * total[:, :, :, 0:3, :]
    finish()
    sent()


def backward_kernel(
    counts, own, part, gpos, gvel, scale, charge,
    ext_ref, gpos_out, gvel_out, charge_out, total, *rest,
):
    landing, sems = rest[:-1], rest[-1]
    near = Neighbours(counts)
    near.greet()
    sent = returned_sum(near, part, total, landing, sems, own)
    grad_position = gpos[...] + total[:, :, :, 0:3, :]
    grad_velocity = gvel[...] + TIME_STEP * grad_position
    finish = spread(near, scale[...] * grad_velocity, ext_ref, sems, own)
    gpos_out[...] = grad_position
    gvel_out[...] = grad_velocity
    charge_out[...] = charge[...] + total[:, :, :, 3:4, :]
    finish()
    sent()


def last_kernel(counts, own, part, gpos, charge, alive, gpos_out, charge_out, total, *rest):
    landing, sems = rest[:-1], rest[-1]
    near = Neighbours(counts)
    near.greet()
    sent = returned_sum(near, part, total, landing, sems, own)
    gpos_out[...] = gpos[...] + total[:, :, :, 0:3, :]
    charge_out[...] = (charge[...] + total[:, :, :, 3:4, :]) * alive[...]
    sent()


def exchange(kernel, identity, own, rows_in, rows_out, *operands):
    counts = tuple(lax.axis_size(axis) for axis in AXES)
    per_block = operands[0].shape[-1]
    extended = tuple(n + 1 for n in own)
    outs = [
        jax.ShapeDtypeStruct((extended if rim else own) + (rows, per_block), jnp.float32)
        for rim, rows in rows_out
    ]
    scratch = []
    if rows_in:
        scratch.append(pltpu.VMEM(own + (rows_in, per_block), jnp.float32))
        for side in SIDES:
            shape = tuple(1 if d else n for d, n in zip(side, own))
            scratch.append(pltpu.VMEM(shape + (rows_in, per_block), jnp.float32))
    scratch.append(pltpu.SemaphoreType.DMA((2, 2 * len(SIDES))))
    vmem = pl.BlockSpec(memory_space=pltpu.VMEM)
    return pl.pallas_call(
        functools.partial(kernel, counts, own),
        out_shape=outs,
        in_specs=[vmem] * len(operands),
        out_specs=[vmem] * len(outs),
        scratch_shapes=scratch,
        compiler_params=pltpu.CompilerParams(
            collective_id=identity, has_side_effects=True, vmem_limit_bytes=4 * 1024 * 1024
        ),
    )(*operands)


def work_kernel(extent, per_block, pair_ref, live_ref, size_ref, place_ref, shift_ref, count_ref):
    extent_y, extent_z = extent

    def coords(index):
        return (index // (extent_y * extent_z), index // extent_z % extent_y, index % extent_z)

    def put(item, rows, lanes, start, shift, weight):
        place_ref[0, item] = rows
        place_ref[1, item] = lanes
        place_ref[2, item] = start
        for axis in range(3):
            shift_ref[axis, item] = shift[axis]
        shift_ref[3, item] = weight

    def one_pair(slot, item):
        first = pair_ref[0, slot]
        second = pair_ref[1, slot]
        swap = size_ref[first] > size_ref[second]
        rows = jnp.where(swap, second, first)
        lanes = jnp.where(swap, first, second)
        weight = jnp.where(first == second, 0.5, 1.0).astype(jnp.float32)
        shift = [
            (one - two).astype(jnp.float32) for one, two in zip(coords(rows), coords(lanes))
        ]
        chunks = (size_ref[rows] + CHUNK - 1) // CHUNK

        def one_chunk(chunk, carry):
            put(item + chunk, rows, lanes, chunk * CHUNK, shift, weight)
            return carry

        lax.fori_loop(0, chunks, one_chunk, 0)
        return item + chunks

    items = lax.fori_loop(0, live_ref[0], one_pair, 0)
    nothing = jnp.float32(0.0)
    for extra in range(BATCH - 1):
        put(items + extra, 0, 0, 0, [nothing] * 3, nothing)
    count_ref[0] = (items + BATCH - 1) // BATCH


def work_list(extent, per_block, sizes, pair_list, pair_count):
    smem = pl.BlockSpec(memory_space=pltpu.SMEM)
    pairs = pair_list[0, 0, 0]
    items = pairs.shape[1] * (per_block // CHUNK) + BATCH
    return pl.pallas_call(
        functools.partial(work_kernel, extent[1:], per_block),
        out_shape=[
            jax.ShapeDtypeStruct((3, items), jnp.int32),
            jax.ShapeDtypeStruct((4, items), jnp.float32),
            jax.ShapeDtypeStruct((1,), jnp.int32),
        ],
        in_specs=[smem] * 3,
        out_specs=[smem] * 3,
        compiler_params=pltpu.CompilerParams(vmem_limit_bytes=4 * 1024 * 1024),
    )(pairs, pair_count.reshape(1), sizes)


def sweep_kernel(force, adjoint, *refs):
    refs = list(refs)
    place_ref, shift_ref, count_ref, pos_ref, par_ref = refs[:5]
    refs = refs[5:]
    cot_ref = refs.pop(0) if adjoint else None
    out_ref, state_ref, column_ref, row_ref, lane_ref = refs
    total, unused, per_block = pos_ref.shape
    rows_out = out_ref.shape[1]
    vectors = rows_out - 1 if adjoint else rows_out
    full = (CHUNK, per_block)

    for block in range(total):
        state_ref[block, 0:3, :] = pos_ref[block]
        state_ref[block, 3:7, :] = par_ref[block]
        if adjoint:
            state_ref[block, 8:11, :] = cot_ref[block]
    for block in range(total):
        column_ref[block] = state_ref[block].T

    def clear(block, carry):
        row_ref[block] = jnp.zeros((rows_out, per_block, per_block), jnp.float32)
        lane_ref[block] = jnp.zeros((rows_out, 8, per_block), jnp.float32)
        return carry

    lax.fori_loop(0, total, clear, 0)

    def item_terms(item):
        rows = place_ref[0, item]
        lanes = place_ref[1, item]
        start = pl.multiple_of(place_ref[2, item], CHUNK)
        weight = shift_ref[3, item]
        columns = column_ref[rows, pl.ds(start, CHUNK), :]

        def lane_row(part):
            return state_ref[lanes, part : part + 1, :]

        def row_column(part):
            return jnp.broadcast_to(columns[:, part : part + 1], full)

        lane_charge = lane_row(3) * (8.0 * weight)
        lane_depth = lane_row(5) * (24.0 * weight)
        d = [row_column(axis) - (lane_row(axis) - shift_ref[axis, item]) for axis in range(3)]
        s = d[0] * d[0] + d[1] * d[1] + d[2] * d[2]
        sigma = row_column(4) + lane_row(4)
        square = sigma * sigma
        inverse = 1.0 / (s + square)
        t = square * inverse
        t3 = t * t * t
        soft = s + SOFT
        r = lax.rsqrt(soft)
        b = jnp.exp(-KAPPA * (soft * r)) * r
        c = jnp.maximum(1.0 - s, 0.0)
        cc = c * c
        p = c * inverse
        y = c * r
        row_charge = row_column(3)
        et = row_column(5) * lane_depth * t3
        below = t3 - 1.0
        twice = t3 + below
        half = 1.0 + 0.5 * r
        k1 = 3.0 + y * half
        charge_b = lane_charge * b
        qb = row_charge * charge_b
        g1 = cc * (et * (below + p * twice) + qb * k1)
        row_terms = []
        if force:
            row_terms += [g1 * d[axis] for axis in range(3)]
        if adjoint:
            h = p * (p * (7.0 * t3 - 2.0) + 3.0 * twice) + below
            k2 = y * (y * (1.0 + r * (1.5 + 0.75 * r)) + 6.0 * half) + 6.0
            k = -2.0 * c * (2.0 * et * h + qb * k2)
            delta = [row_column(8 + axis) - lane_row(8 + axis) for axis in range(3)]
            along = delta[0] * d[0] + delta[1] * d[1] + delta[2] * d[2]
            ka = k * along
            row_terms += [g1 * delta[axis] + ka * d[axis] for axis in range(3)]

        def folded(value):
            return functools.reduce(
                lambda one, two: one + two,
                [value[8 * group : 8 * group + 8] for group in range(CHUNK // 8)],
            )

        lane_terms = [-folded(value) for value in row_terms]
        if adjoint:
            m = cc * k1 * along
            row_terms.append(m * charge_b)
            lane_terms.append(folded(m * b * row_charge) * (8.0 * weight))
        return (rows, lanes, start, row_terms, lane_terms)

    def one_batch(batch, carry):
        found = [item_terms(batch * BATCH + index) for index in range(BATCH)]
        for rows, lanes, start, row_terms, lane_terms in found:
            where = pl.ds(start, CHUNK)
            old_rows = [row_ref[rows, part, where, :] for part in range(rows_out)]
            old_lanes = [lane_ref[lanes, part] for part in range(rows_out)]
            for part in range(rows_out):
                row_ref[rows, part, where, :] = old_rows[part] + row_terms[part]
                lane_ref[lanes, part] = old_lanes[part] + lane_terms[part]
        return carry

    lax.fori_loop(0, count_ref[0], one_batch, 0)

    which = lax.broadcasted_iota(jnp.int32, (per_block, 8), 1)
    for block in range(total):
        columns = jnp.zeros((per_block, 8), jnp.float32)
        for part in range(rows_out):
            summed = jnp.sum(row_ref[block, part], axis=1, keepdims=True)
            columns = jnp.where(which == part, summed, columns)
        turned = columns.T
        sums = [jnp.sum(lane_ref[block, part], axis=0, keepdims=True) for part in range(rows_out)]
        out_ref[block] = turned[0:rows_out] + jnp.concatenate(sums, axis=0)


def sweep(ext_pos, ext_par, work, ext_cot, force):
    extent = ext_pos.shape[:3]
    per_block = ext_pos.shape[-1]
    total = extent[0] * extent[1] * extent[2]
    adjoint = ext_cot is not None
    rows_out = (3 if force else 0) + (4 if adjoint else 0)
    operands = list(work) + [ext_pos.reshape(total, 3, per_block), ext_par]
    if adjoint:
        operands.append(ext_cot.reshape(total, 3, per_block))
    smem = pl.BlockSpec(memory_space=pltpu.SMEM)
    vmem = pl.BlockSpec(memory_space=pltpu.VMEM)
    height = 16 if adjoint else 8
    out = pl.pallas_call(
        functools.partial(sweep_kernel, force, adjoint),
        out_shape=jax.ShapeDtypeStruct((total, rows_out, per_block), jnp.float32),
        in_specs=[smem] * 3 + [vmem] * (len(operands) - 3),
        out_specs=vmem,
        scratch_shapes=[
            pltpu.VMEM((total, height, per_block), jnp.float32),
            pltpu.VMEM((total, per_block, height), jnp.float32),
            pltpu.VMEM((total, rows_out, per_block, per_block), jnp.float32),
            pltpu.VMEM((total, rows_out, 8, per_block), jnp.float32),
        ],
        compiler_params=pltpu.CompilerParams(vmem_limit_bytes=40 * 1024 * 1024),
    )(*operands)
    return out.reshape(extent + (rows_out, per_block))


def on_device(
    positions,
    velocities,
    charges,
    atom_types,
    atom_count,
    sigma_type,
    epsilon_type,
    masses,
    pair_list,
    pair_count,
    pos_cotangent,
    vel_cotangent,
):
    alive_mask, params = atom_params(charges, atom_types, atom_count, sigma_type, epsilon_type)
    inverse = (1.0 / masses)[..., None, :]
    half_step = 0.5 * TIME_STEP
    own = positions.shape[:3]
    per_block = positions.shape[-1]
    half_scale = jnp.broadcast_to(half_step * inverse, positions.shape)
    full_scale = jnp.broadcast_to(TIME_STEP * inverse, positions.shape)
    field = jnp.concatenate([positions, params, half_scale * vel_cotangent], axis=3)
    (extended,) = exchange(first_kernel, 1, own, 0, [(True, 10)], field)
    ext_par = extended[:, :, :, 3:7].reshape(-1, 4, per_block)
    last_cot = extended[:, :, :, 7:10]
    sizes = jnp.sum(ext_par[:, 3], axis=-1).astype(jnp.int32)
    work = work_list(extended.shape[:3], per_block, sizes, pair_list, pair_count)
    history = [extended[:, :, :, :3]]
    velocity = velocities
    for step_index in range(STEPS):
        part = sweep(history[-1], ext_par, work, None, True)
        scale = half_scale if step_index == 0 else full_scale
        ext_next, velocity = exchange(
            forward_kernel, 2, own, 3, [(True, 3), (False, 3)], part, history[-1], velocity, scale
        )
        history.append(ext_next)
    part = sweep(history[STEPS], ext_par, work, last_cot, True)
    ext_cot, grad_position, grad_velocity, charge_sum, velocity = exchange(
        turn_kernel,
        3,
        own,
        7,
        [(True, 3), (False, 3), (False, 3), (False, 1), (False, 3)],
        part,
        velocity,
        half_scale,
        pos_cotangent,
        vel_cotangent,
        full_scale,
    )
    for step_index in range(STEPS - 1, 0, -1):
        part = sweep(history[step_index], ext_par, work, ext_cot, False)
        scale = full_scale if step_index > 1 else half_scale
        ext_cot, grad_position, grad_velocity, charge_sum = exchange(
            backward_kernel,
            4,
            own,
            4,
            [(True, 3), (False, 3), (False, 3), (False, 1)],
            part,
            grad_position,
            grad_velocity,
            scale,
            charge_sum,
        )
    part = sweep(history[0], ext_par, work, ext_cot, False)
    grad_position, charge_sum = exchange(
        last_kernel,
        5,
        own,
        4,
        [(False, 3), (False, 1)],
        part,
        grad_position,
        charge_sum,
        alive_mask[..., None, :],
    )
    position = history[STEPS][: own[0], : own[1], : own[2]]
    return (position, velocity, grad_position, grad_velocity, charge_sum[:, :, :, 0])


def solution(mesh):
    in_specs = (
        P("gx", "gy", "gz", None, None),
        P("gx", "gy", "gz", None, None),
        P("gx", "gy", "gz", None),
        P("gx", "gy", "gz", None),
        P("gx", "gy", "gz"),
        P(),
        P(),
        P("gx", "gy", "gz", None),
        P("gx", "gy", "gz", None, None),
        P("gx", "gy", "gz"),
        P("gx", "gy", "gz", None, None),
        P("gx", "gy", "gz", None, None),
    )
    out_specs = (
        P("gx", "gy", "gz", None, None),
        P("gx", "gy", "gz", None, None),
        P("gx", "gy", "gz", None, None),
        P("gx", "gy", "gz", None, None),
        P("gx", "gy", "gz", None),
    )
    return jax.shard_map(
        on_device, mesh=mesh, in_specs=in_specs, out_specs=out_specs, check_vma=False
    )
```

```python
import functools

import jax
import jax.numpy as jnp
from jax import lax
from jax.experimental import pallas as pl
from jax.experimental.pallas import tpu as pltpu
from jax.sharding import PartitionSpec as P

STEPS = 5


SOFT = 0.04
KAPPA = 2.0
TIME_STEP = 0.004
CHUNK = 16
BATCH = 8


def atom_params(charges, atom_types, atom_count, sigma_type, epsilon_type):
    type_total = sigma_type.shape[0]
    alive_mask = (
        lax.broadcasted_iota(jnp.int32, charges.shape, charges.ndim - 1) < atom_count[..., None]
    ).astype(jnp.float32)
    matches = (
        atom_types[..., None, :] == lax.broadcasted_iota(jnp.int32, (type_total, 1), 0)
    ).astype(jnp.float32)
    sigma_atom = jnp.sum(matches * sigma_type[:, None], axis=-2)
    depth_atom = jnp.sum(matches * epsilon_type[:, None], axis=-2)
    params = jnp.stack(
        [charges * alive_mask, 0.5 * sigma_atom, jnp.sqrt(depth_atom) * alive_mask, alive_mask],
        axis=-2,
    )
    return (alive_mask, params)


AXES = ("gx", "gy", "gz")
SIDES = [(x, y, z) for x in (0, 1) for y in (0, 1) for z in (0, 1)][1:]


def low_part(side, own):
    return tuple(pl.ds(0, 1 if d else n) for d, n in zip(side, own))


def rim_part(side, own):
    return tuple(pl.ds(n, 1) if d else pl.ds(0, n) for d, n in zip(side, own))


class Neighbours:
    def __init__(self, counts):
        self.counts = counts
        self.here = tuple(lax.axis_index(axis) for axis in AXES)

    def at(self, side, sign):
        return tuple(place + sign * step for place, step in zip(self.here, side))

    def exists(self, side, sign):
        found = None
        for place, step, count in zip(self.here, side, self.counts):
            if step:
                test = place < count - 1 if sign > 0 else place > 0
                found = test if found is None else jnp.logical_and(found, test)
        return found

    def greet(self):
        barrier = pltpu.get_barrier_semaphore()
        for sign in (1, -1):
            for side in SIDES:

                @pl.when(self.exists(side, sign))
                def _(side=side, sign=sign):
                    pl.semaphore_signal(
                        barrier,
                        inc=1,
                        device_id=self.at(side, sign),
                        device_id_type=pl.DeviceIdType.MESH,
                    )

        peers = sum(
            self.exists(side, sign).astype(jnp.int32) for sign in (1, -1) for side in SIDES
        )
        pl.semaphore_wait(barrier, peers)

    def copy(self, source, target, sems, index, side, sign):
        return pltpu.make_async_remote_copy(
            src_ref=source,
            dst_ref=target,
            send_sem=sems.at[0, index],
            recv_sem=sems.at[1, index],
            device_id=self.at(side, sign),
            device_id_type=pl.DeviceIdType.MESH,
        )


def returned_sum(near, part_ref, total_ref, landing, sems, own):
    def moved(index, side):
        return near.copy(
            part_ref.at[rim_part(side, own)], landing[index], sems, index, side, 1
        )

    for index, side in enumerate(SIDES):

        @pl.when(near.exists(side, 1))
        def _(index=index, side=side):
            moved(index, side).start()

    total_ref[...] = part_ref[tuple(pl.ds(0, n) for n in own)]
    for index, side in enumerate(SIDES):

        @pl.when(near.exists(side, -1))
        def _(index=index, side=side):
            moved(index, side).wait_recv()
            where = low_part(side, own)
            total_ref[where] = total_ref[where] + landing[index][...]

    def finish():
        for index, side in enumerate(SIDES):

            @pl.when(near.exists(side, 1))
            def _(index=index, side=side):
                moved(index, side).wait_send()

    return finish


def spread(near, value, ext_ref, sems, own):
    ext_ref[tuple(pl.ds(0, n) for n in own)] = value
    base = len(SIDES)

    def moved(index, side):
        return near.copy(
            ext_ref.at[low_part(side, own)],
            ext_ref.at[rim_part(side, own)],
            sems,
            base + index,
            side,
            -1,
        )

    for index, side in enumerate(SIDES):

        @pl.when(near.exists(side, -1))
        def _(index=index, side=side):
            moved(index, side).start()

    for index, side in enumerate(SIDES):

        @pl.when(jnp.logical_not(near.exists(side, 1)))
        def _(index=index, side=side):
            where = rim_part(side, own)
            shape = tuple(1 if d else n for d, n in zip(side, own)) + ext_ref.shape[3:]
            ext_ref[where] = jnp.zeros(shape, jnp.float32)

    def finish():
        for index, side in enumerate(SIDES):

            @pl.when(near.exists(side, 1))
            def _(index=index, side=side):
                moved(index, side).wait_recv()

        for index, side in enumerate(SIDES):

            @pl.when(near.exists(side, -1))
            def _(index=index, side=side):
                moved(index, side).wait_send()

    return finish


def first_kernel(counts, own, field_ref, ext_ref, sems):
    near = Neighbours(counts)
    near.greet()
    spread(near, field_ref[...], ext_ref, sems, own)()


def forward_kernel(counts, own, part, ext_old, vel, scale, ext_ref, vel_out, total, *rest):
    landing, sems = rest[:-1], rest[-1]
    near = Neighbours(counts)
    near.greet()
    sent = returned_sum(near, part, total, landing, sems, own)
    velocity = vel[...] + scale[...] * total[...]
    vel_out[...] = velocity
    position = ext_old[tuple(pl.ds(0, n) for n in own)] + TIME_STEP * velocity
    spread(near, position, ext_ref, sems, own)()
    sent()


def turn_kernel(
    counts, own, part, vel, vel_scale, gpos, gvel, scale,
    ext_ref, gpos_out, gvel_out, charge_out, vel_out, total, *rest,
):
    landing, sems = rest[:-1], rest[-1]
    near = Neighbours(counts)
    near.greet()
    sent = returned_sum(near, part, total, landing, sems, own)
    grad_position = gpos[...] + total[:, :, :, 3:6, :]
    grad_velocity = gvel[...] + TIME_STEP * grad_position
    finish = spread(near, scale[...] * grad_velocity, ext_ref, sems, own)
    gpos_out[...] = grad_position
    gvel_out[...] = grad_velocity
    charge_out[...] = total[:, :, :, 6:7, :]
    vel_out[...] = vel[...] + vel_scale[...] * total[:, :, :, 0:3, :]
    finish()
    sent()


def backward_kernel(
    counts, own, part, gpos, gvel, scale, charge,
    ext_ref, gpos_out, gvel_out, charge_out, total, *rest,
):
    landing, sems = rest[:-1], rest[-1]
    near = Neighbours(counts)
    near.greet()
    sent = returned_sum(near, part, total, landing, sems, own)
    grad_position = gpos[...] + total[:, :, :, 0:3, :]
    grad_velocity = gvel[...] + TIME_STEP * grad_position
    finish = spread(near, scale[...] * grad_velocity, ext_ref, sems, own)
    gpos_out[...] = grad_position
    gvel_out[...] = grad_velocity
    charge_out[...] = charge[...] + total[:, :, :, 3:4, :]
    finish()
    sent()


def last_kernel(counts, own, part, gpos, charge, alive, gpos_out, charge_out, total, *rest):
    landing, sems = rest[:-1], rest[-1]
    near = Neighbours(counts)
    near.greet()
    sent = returned_sum(near, part, total, landing, sems, own)
    gpos_out[...] = gpos[...] + total[:, :, :, 0:3, :]
    charge_out[...] = (charge[...] + total[:, :, :, 3:4, :]) * alive[...]
    sent()


def exchange(kernel, identity, own, rows_in, rows_out, *operands):
    counts = tuple(lax.axis_size(axis) for axis in AXES)
    per_block = operands[0].shape[-1]
    extended = tuple(n + 1 for n in own)
    outs = [
        jax.ShapeDtypeStruct((extended if rim else own) + (rows, per_block), jnp.float32)
        for rim, rows in rows_out
    ]
    scratch = []
    if rows_in:
        scratch.append(pltpu.VMEM(own + (rows_in, per_block), jnp.float32))
        for side in SIDES:
            shape = tuple(1 if d else n for d, n in zip(side, own))
            scratch.append(pltpu.VMEM(shape + (rows_in, per_block), jnp.float32))
    scratch.append(pltpu.SemaphoreType.DMA((2, 2 * len(SIDES))))
    vmem = pl.BlockSpec(memory_space=pltpu.VMEM)
    return pl.pallas_call(
        functools.partial(kernel, counts, own),
        out_shape=outs,
        in_specs=[vmem] * len(operands),
        out_specs=[vmem] * len(outs),
        scratch_shapes=scratch,
        compiler_params=pltpu.CompilerParams(
            collective_id=identity, has_side_effects=True, vmem_limit_bytes=4 * 1024 * 1024
        ),
    )(*operands)


def work_kernel(
    extent, per_block, pair_ref, live_ref, size_ref, item_ref, table_ref, shift_ref, count_ref
):
    extent_y, extent_z = extent

    def coords(index):
        return (index // (extent_y * extent_z), index // extent_z % extent_y, index % extent_z)

    slots = pair_ref.shape[1]
    steps = per_block // CHUNK

    def one_pair(slot, item):
        first = pair_ref[0, slot]
        second = pair_ref[1, slot]
        swap = size_ref[first] > size_ref[second]
        rows = jnp.where(swap, second, first)
        lanes = jnp.where(swap, first, second)
        table_ref[0, slot] = rows
        table_ref[1, slot] = lanes
        for axis, (one, two) in enumerate(zip(coords(rows), coords(lanes))):
            shift_ref[axis, slot] = (one - two).astype(jnp.float32)
        shift_ref[3, slot] = jnp.where(first == second, 0.5, 1.0).astype(jnp.float32)
        for step in range(steps):
            item_ref[item + step] = slot * steps + step
        return item + (size_ref[rows] + CHUNK - 1) // CHUNK

    items = lax.fori_loop(0, live_ref[0], one_pair, 0)
    for row in range(2):
        table_ref[row, slots] = 0
    for row in range(4):
        shift_ref[row, slots] = jnp.float32(0.0)
    for extra in range(BATCH - 1):
        item_ref[items + extra] = slots * steps
    count_ref[0] = (items + BATCH - 1) // BATCH


def work_list(extent, per_block, sizes, pair_list, pair_count):
    smem = pl.BlockSpec(memory_space=pltpu.SMEM)
    pairs = pair_list[0, 0, 0]
    slots = pairs.shape[1]
    steps = per_block // CHUNK
    return pl.pallas_call(
        functools.partial(work_kernel, extent[1:], per_block),
        out_shape=[
            jax.ShapeDtypeStruct(((slots + 1) * steps + BATCH,), jnp.int32),
            jax.ShapeDtypeStruct((2, slots + 1), jnp.int32),
            jax.ShapeDtypeStruct((4, slots + 1), jnp.float32),
            jax.ShapeDtypeStruct((1,), jnp.int32),
        ],
        in_specs=[smem] * 3,
        out_specs=[smem] * 4,
        compiler_params=pltpu.CompilerParams(vmem_limit_bytes=4 * 1024 * 1024),
    )(pairs, pair_count.reshape(1), sizes)


def sweep_kernel(force, adjoint, *refs):
    refs = list(refs)
    item_ref, table_ref, shift_ref, count_ref, pos_ref, par_ref = refs[:6]
    refs = refs[6:]
    cot_ref = refs.pop(0) if adjoint else None
    out_ref, state_ref, column_ref, row_ref, lane_ref = refs
    total, unused, per_block = pos_ref.shape
    rows_out = out_ref.shape[1]
    vectors = rows_out - 1 if adjoint else rows_out
    full = (CHUNK, per_block)
    steps = per_block // CHUNK

    for block in range(total):
        state_ref[block, 0:3, :] = pos_ref[block]
        state_ref[block, 3:7, :] = par_ref[block]
        if adjoint:
            state_ref[block, 8:11, :] = cot_ref[block]
    for block in range(total):
        column_ref[block] = state_ref[block].T

    def clear(block, carry):
        row_ref[block] = jnp.zeros((rows_out, per_block, per_block), jnp.float32)
        lane_ref[block] = jnp.zeros((rows_out, 8, per_block), jnp.float32)
        return carry

    lax.fori_loop(0, total, clear, 0)

    def item_terms(item):
        packed = item_ref[item]
        slot = packed // steps
        rows = table_ref[0, slot]
        lanes = table_ref[1, slot]
        start = pl.multiple_of((packed - slot * steps) * CHUNK, CHUNK)
        weight = shift_ref[3, slot]
        columns = column_ref[rows, pl.ds(start, CHUNK), :]

        def lane_row(part):
            return state_ref[lanes, part : part + 1, :]

        def row_column(part):
            return jnp.broadcast_to(columns[:, part : part + 1], full)

        lane_charge = lane_row(3) * (8.0 * weight)
        lane_depth = lane_row(5) * (24.0 * weight)
        d = [row_column(axis) - (lane_row(axis) - shift_ref[axis, slot]) for axis in range(3)]
        s = d[0] * d[0] + d[1] * d[1] + d[2] * d[2]
        sigma = row_column(4) + lane_row(4)
        square = sigma * sigma
        inverse = 1.0 / (s + square)
        t = square * inverse
        t3 = t * t * t
        soft = s + SOFT
        r = lax.rsqrt(soft)
        b = jnp.exp(-KAPPA * (soft * r)) * r
        c = jnp.maximum(1.0 - s, 0.0)
        cc = c * c
        p = c * inverse
        y = c * r
        row_charge = row_column(3)
        et = row_column(5) * lane_depth * t3
        below = t3 - 1.0
        twice = t3 + below
        half = 1.0 + 0.5 * r
        k1 = 3.0 + y * half
        charge_b = lane_charge * b
        qb = row_charge * charge_b
        g1 = cc * (et * (below + p * twice) + qb * k1)
        row_terms = []
        if force:
            row_terms += [g1 * d[axis] for axis in range(3)]
        if adjoint:
            h = p * (p * (7.0 * t3 - 2.0) + 3.0 * twice) + below
            k2 = y * (y * (1.0 + r * (1.5 + 0.75 * r)) + 6.0 * half) + 6.0
            k = -2.0 * c * (2.0 * et * h + qb * k2)
            delta = [row_column(8 + axis) - lane_row(8 + axis) for axis in range(3)]
            along = delta[0] * d[0] + delta[1] * d[1] + delta[2] * d[2]
            ka = k * along
            row_terms += [g1 * delta[axis] + ka * d[axis] for axis in range(3)]

        def folded(value):
            return functools.reduce(
                lambda one, two: one + two,
                [value[8 * group : 8 * group + 8] for group in range(CHUNK // 8)],
            )

        lane_terms = [-folded(value) for value in row_terms]
        if adjoint:
            m = cc * k1 * along
            row_terms.append(m * charge_b)
            lane_terms.append(folded(m * b * row_charge) * (8.0 * weight))
        return (rows, lanes, start, row_terms, lane_terms)

    def one_batch(batch, carry):
        found = [item_terms(batch * BATCH + index) for index in range(BATCH)]
        for rows, lanes, start, row_terms, lane_terms in found:
            where = pl.ds(start, CHUNK)
            old_rows = [row_ref[rows, part, where, :] for part in range(rows_out)]
            old_lanes = [lane_ref[lanes, part] for part in range(rows_out)]
            for part in range(rows_out):
                row_ref[rows, part, where, :] = old_rows[part] + row_terms[part]
                lane_ref[lanes, part] = old_lanes[part] + lane_terms[part]
        return carry

    lax.fori_loop(0, count_ref[0], one_batch, 0)

    which = lax.broadcasted_iota(jnp.int32, (per_block, 8), 1)
    for block in range(total):
        columns = jnp.zeros((per_block, 8), jnp.float32)
        for part in range(rows_out):
            summed = jnp.sum(row_ref[block, part], axis=1, keepdims=True)
            columns = jnp.where(which == part, summed, columns)
        turned = columns.T
        sums = [jnp.sum(lane_ref[block, part], axis=0, keepdims=True) for part in range(rows_out)]
        out_ref[block] = turned[0:rows_out] + jnp.concatenate(sums, axis=0)


def sweep(ext_pos, ext_par, work, ext_cot, force):
    extent = ext_pos.shape[:3]
    per_block = ext_pos.shape[-1]
    total = extent[0] * extent[1] * extent[2]
    adjoint = ext_cot is not None
    rows_out = (3 if force else 0) + (4 if adjoint else 0)
    operands = list(work) + [ext_pos.reshape(total, 3, per_block), ext_par]
    if adjoint:
        operands.append(ext_cot.reshape(total, 3, per_block))
    smem = pl.BlockSpec(memory_space=pltpu.SMEM)
    vmem = pl.BlockSpec(memory_space=pltpu.VMEM)
    height = 16 if adjoint else 8
    out = pl.pallas_call(
        functools.partial(sweep_kernel, force, adjoint),
        out_shape=jax.ShapeDtypeStruct((total, rows_out, per_block), jnp.float32),
        in_specs=[smem] * 4 + [vmem] * (len(operands) - 4),
        out_specs=vmem,
        scratch_shapes=[
            pltpu.VMEM((total, height, per_block), jnp.float32),
            pltpu.VMEM((total, per_block, height), jnp.float32),
            pltpu.VMEM((total, rows_out, per_block, per_block), jnp.float32),
            pltpu.VMEM((total, rows_out, 8, per_block), jnp.float32),
        ],
        compiler_params=pltpu.CompilerParams(vmem_limit_bytes=40 * 1024 * 1024),
    )(*operands)
    return out.reshape(extent + (rows_out, per_block))


def on_device(
    positions,
    velocities,
    charges,
    atom_types,
    atom_count,
    sigma_type,
    epsilon_type,
    masses,
    pair_list,
    pair_count,
    pos_cotangent,
    vel_cotangent,
):
    alive_mask, params = atom_params(charges, atom_types, atom_count, sigma_type, epsilon_type)
    inverse = (1.0 / masses)[..., None, :]
    half_step = 0.5 * TIME_STEP
    own = positions.shape[:3]
    per_block = positions.shape[-1]
    half_scale = jnp.broadcast_to(half_step * inverse, positions.shape)
    full_scale = jnp.broadcast_to(TIME_STEP * inverse, positions.shape)
    field = jnp.concatenate([positions, params, half_scale * vel_cotangent], axis=3)
    (extended,) = exchange(first_kernel, 1, own, 0, [(True, 10)], field)
    ext_par = extended[:, :, :, 3:7].reshape(-1, 4, per_block)
    last_cot = extended[:, :, :, 7:10]
    sizes = jnp.sum(ext_par[:, 3], axis=-1).astype(jnp.int32)
    work = work_list(extended.shape[:3], per_block, sizes, pair_list, pair_count)
    history = [extended[:, :, :, :3]]
    velocity = velocities
    for step_index in range(STEPS):
        part = sweep(history[-1], ext_par, work, None, True)
        scale = half_scale if step_index == 0 else full_scale
        ext_next, velocity = exchange(
            forward_kernel, 2, own, 3, [(True, 3), (False, 3)], part, history[-1], velocity, scale
        )
        history.append(ext_next)
    part = sweep(history[STEPS], ext_par, work, last_cot, True)
    ext_cot, grad_position, grad_velocity, charge_sum, velocity = exchange(
        turn_kernel,
        3,
        own,
        7,
        [(True, 3), (False, 3), (False, 3), (False, 1), (False, 3)],
        part,
        velocity,
        half_scale,
        pos_cotangent,
        vel_cotangent,
        full_scale,
    )
    for step_index in range(STEPS - 1, 0, -1):
        part = sweep(history[step_index], ext_par, work, ext_cot, False)
        scale = full_scale if step_index > 1 else half_scale
        ext_cot, grad_position, grad_velocity, charge_sum = exchange(
            backward_kernel,
            4,
            own,
            4,
            [(True, 3), (False, 3), (False, 3), (False, 1)],
            part,
            grad_position,
            grad_velocity,
            scale,
            charge_sum,
        )
    part = sweep(history[0], ext_par, work, ext_cot, False)
    grad_position, charge_sum = exchange(
        last_kernel,
        5,
        own,
        4,
        [(False, 3), (False, 1)],
        part,
        grad_position,
        charge_sum,
        alive_mask[..., None, :],
    )
    position = history[STEPS][: own[0], : own[1], : own[2]]
    return (position, velocity, grad_position, grad_velocity, charge_sum[:, :, :, 0])


def solution(mesh):
    in_specs = (
        P("gx", "gy", "gz", None, None),
        P("gx", "gy", "gz", None, None),
        P("gx", "gy", "gz", None),
        P("gx", "gy", "gz", None),
        P("gx", "gy", "gz"),
        P(),
        P(),
        P("gx", "gy", "gz", None),
        P("gx", "gy", "gz", None, None),
        P("gx", "gy", "gz"),
        P("gx", "gy", "gz", None, None),
        P("gx", "gy", "gz", None, None),
    )
    out_specs = (
        P("gx", "gy", "gz", None, None),
        P("gx", "gy", "gz", None, None),
        P("gx", "gy", "gz", None, None),
        P("gx", "gy", "gz", None, None),
        P("gx", "gy", "gz", None),
    )
    return jax.shard_map(
        on_device, mesh=mesh, in_specs=in_specs, out_specs=out_specs, check_vma=False
    )
```

```python
import functools
import math

import jax
import jax.numpy as jnp
from jax import lax
from jax.experimental import pallas as pl
from jax.experimental.pallas import tpu as pltpu
from jax.sharding import PartitionSpec as P

STEPS = 5


SOFT = 0.04
KAPPA = 2.0
EXPONENT = -KAPPA / math.log(2.0)
TIME_STEP = 0.004
CHUNK = 16
BATCH = 8


def atom_params(charges, atom_types, atom_count, sigma_type, epsilon_type):
    type_total = sigma_type.shape[0]
    alive_mask = (
        lax.broadcasted_iota(jnp.int32, charges.shape, charges.ndim - 1) < atom_count[..., None]
    ).astype(jnp.float32)
    matches = (
        atom_types[..., None, :] == lax.broadcasted_iota(jnp.int32, (type_total, 1), 0)
    ).astype(jnp.float32)
    sigma_atom = jnp.sum(matches * sigma_type[:, None], axis=-2)
    depth_atom = jnp.sum(matches * epsilon_type[:, None], axis=-2)
    params = jnp.stack(
        [charges * alive_mask, 0.5 * sigma_atom, jnp.sqrt(depth_atom) * alive_mask, alive_mask],
        axis=-2,
    )
    return (alive_mask, params)


AXES = ("gx", "gy", "gz")
SIDES = sorted(
    [(x, y, z) for x in (0, 1) for y in (0, 1) for z in (0, 1)][1:], key=sum, reverse=True
)


def low_part(side, own):
    return tuple(pl.ds(0, 1 if d else n) for d, n in zip(side, own))


def rim_part(side, own):
    return tuple(pl.ds(n, 1) if d else pl.ds(0, n) for d, n in zip(side, own))


class Neighbours:
    def __init__(self, counts):
        self.counts = counts
        self.here = tuple(lax.axis_index(axis) for axis in AXES)

    def at(self, side, sign):
        return tuple(place + sign * step for place, step in zip(self.here, side))

    def exists(self, side, sign):
        found = None
        for place, step, count in zip(self.here, side, self.counts):
            if step:
                test = place < count - 1 if sign > 0 else place > 0
                found = test if found is None else jnp.logical_and(found, test)
        return found

    def greet(self):
        barrier = pltpu.get_barrier_semaphore()
        for sign in (1, -1):
            for side in SIDES:

                @pl.when(self.exists(side, sign))
                def _(side=side, sign=sign):
                    pl.semaphore_signal(
                        barrier,
                        inc=1,
                        device_id=self.at(side, sign),
                        device_id_type=pl.DeviceIdType.MESH,
                    )

        peers = sum(
            self.exists(side, sign).astype(jnp.int32) for sign in (1, -1) for side in SIDES
        )
        pl.semaphore_wait(barrier, peers)

    def copy(self, source, target, sems, index, side, sign):
        return pltpu.make_async_remote_copy(
            src_ref=source,
            dst_ref=target,
            send_sem=sems.at[0, index],
            recv_sem=sems.at[1, index],
            device_id=self.at(side, sign),
            device_id_type=pl.DeviceIdType.MESH,
        )


def returned_sum(near, part_ref, total_ref, landing, sems, own):
    def moved(index, side):
        return near.copy(
            part_ref.at[rim_part(side, own)], landing[index], sems, index, side, 1
        )

    for index, side in enumerate(SIDES):

        @pl.when(near.exists(side, 1))
        def _(index=index, side=side):
            moved(index, side).start()

    total_ref[...] = part_ref[tuple(pl.ds(0, n) for n in own)]
    for index, side in enumerate(SIDES):

        @pl.when(near.exists(side, -1))
        def _(index=index, side=side):
            moved(index, side).wait_recv()
            where = low_part(side, own)
            total_ref[where] = total_ref[where] + landing[index][...]

    def finish():
        for index, side in enumerate(SIDES):

            @pl.when(near.exists(side, 1))
            def _(index=index, side=side):
                moved(index, side).wait_send()

    return finish


def spread(near, value, ext_ref, sems, own):
    ext_ref[tuple(pl.ds(0, n) for n in own)] = value
    base = len(SIDES)

    def moved(index, side):
        return near.copy(
            ext_ref.at[low_part(side, own)],
            ext_ref.at[rim_part(side, own)],
            sems,
            base + index,
            side,
            -1,
        )

    for index, side in enumerate(SIDES):

        @pl.when(near.exists(side, -1))
        def _(index=index, side=side):
            moved(index, side).start()

    for index, side in enumerate(SIDES):

        @pl.when(jnp.logical_not(near.exists(side, 1)))
        def _(index=index, side=side):
            where = rim_part(side, own)
            shape = tuple(1 if d else n for d, n in zip(side, own)) + ext_ref.shape[3:]
            ext_ref[where] = jnp.zeros(shape, jnp.float32)

    def finish():
        for index, side in enumerate(SIDES):

            @pl.when(near.exists(side, 1))
            def _(index=index, side=side):
                moved(index, side).wait_recv()

        for index, side in enumerate(SIDES):

            @pl.when(near.exists(side, -1))
            def _(index=index, side=side):
                moved(index, side).wait_send()

    return finish


def first_kernel(counts, own, field_ref, ext_ref, sems):
    near = Neighbours(counts)
    near.greet()
    spread(near, field_ref[...], ext_ref, sems, own)()


def forward_kernel(counts, own, part, ext_old, vel, scale, ext_ref, vel_out, total, *rest):
    landing, sems = rest[:-1], rest[-1]
    near = Neighbours(counts)
    near.greet()
    sent = returned_sum(near, part, total, landing, sems, own)
    velocity = vel[...] + scale[...] * total[...]
    vel_out[...] = velocity
    position = ext_old[tuple(pl.ds(0, n) for n in own)] + TIME_STEP * velocity
    spread(near, position, ext_ref, sems, own)()
    sent()


def turn_kernel(
    counts, own, part, vel, vel_scale, gpos, gvel, scale,
    ext_ref, gpos_out, gvel_out, charge_out, vel_out, total, *rest,
):
    landing, sems = rest[:-1], rest[-1]
    near = Neighbours(counts)
    near.greet()
    sent = returned_sum(near, part, total, landing, sems, own)
    grad_position = gpos[...] + total[:, :, :, 3:6, :]
    grad_velocity = gvel[...] + TIME_STEP * grad_position
    finish = spread(near, scale[...] * grad_velocity, ext_ref, sems, own)
    gpos_out[...] = grad_position
    gvel_out[...] = grad_velocity
    charge_out[...] = total[:, :, :, 6:7, :]
    vel_out[...] = vel[...] + vel_scale[...] * total[:, :, :, 0:3, :]
    finish()
    sent()


def backward_kernel(
    counts, own, part, gpos, gvel, scale, charge,
    ext_ref, gpos_out, gvel_out, charge_out, total, *rest,
):
    landing, sems = rest[:-1], rest[-1]
    near = Neighbours(counts)
    near.greet()
    sent = returned_sum(near, part, total, landing, sems, own)
    grad_position = gpos[...] + total[:, :, :, 0:3, :]
    grad_velocity = gvel[...] + TIME_STEP * grad_position
    finish = spread(near, scale[...] * grad_velocity, ext_ref, sems, own)
    gpos_out[...] = grad_position
    gvel_out[...] = grad_velocity
    charge_out[...] = charge[...] + total[:, :, :, 3:4, :]
    finish()
    sent()


def last_kernel(counts, own, part, gpos, charge, alive, gpos_out, charge_out, total, *rest):
    landing, sems = rest[:-1], rest[-1]
    near = Neighbours(counts)
    near.greet()
    sent = returned_sum(near, part, total, landing, sems, own)
    gpos_out[...] = gpos[...] + total[:, :, :, 0:3, :]
    charge_out[...] = (charge[...] + total[:, :, :, 3:4, :]) * alive[...]
    sent()


def exchange(kernel, identity, own, rows_in, rows_out, *operands):
    counts = tuple(lax.axis_size(axis) for axis in AXES)
    per_block = operands[0].shape[-1]
    extended = tuple(n + 1 for n in own)
    outs = [
        jax.ShapeDtypeStruct((extended if rim else own) + (rows, per_block), jnp.float32)
        for rim, rows in rows_out
    ]
    scratch = []
    if rows_in:
        scratch.append(pltpu.VMEM(own + (rows_in, per_block), jnp.float32))
        for side in SIDES:
            shape = tuple(1 if d else n for d, n in zip(side, own))
            scratch.append(pltpu.VMEM(shape + (rows_in, per_block), jnp.float32))
    scratch.append(pltpu.SemaphoreType.DMA((2, 2 * len(SIDES))))
    vmem = pl.BlockSpec(memory_space=pltpu.VMEM)
    return pl.pallas_call(
        functools.partial(kernel, counts, own),
        out_shape=outs,
        in_specs=[vmem] * len(operands),
        out_specs=[vmem] * len(outs),
        scratch_shapes=scratch,
        compiler_params=pltpu.CompilerParams(
            collective_id=identity, has_side_effects=True, vmem_limit_bytes=4 * 1024 * 1024
        ),
    )(*operands)


def work_kernel(
    extent, per_block, pair_ref, live_ref, size_ref, item_ref, table_ref, shift_ref, count_ref
):
    extent_y, extent_z = extent

    def coords(index):
        return (index // (extent_y * extent_z), index // extent_z % extent_y, index % extent_z)

    slots = pair_ref.shape[1]
    steps = per_block // CHUNK

    def one_pair(slot, item):
        first = pair_ref[0, slot]
        second = pair_ref[1, slot]
        swap = size_ref[first] > size_ref[second]
        rows = jnp.where(swap, second, first)
        lanes = jnp.where(swap, first, second)
        table_ref[0, slot] = rows
        table_ref[1, slot] = lanes
        for axis, (one, two) in enumerate(zip(coords(rows), coords(lanes))):
            shift_ref[axis, slot] = (one - two).astype(jnp.float32)
        shift_ref[3, slot] = jnp.where(first == second, 0.5, 1.0).astype(jnp.float32)
        for step in range(steps):
            item_ref[item + step] = slot * steps + step
        return item + (size_ref[rows] + CHUNK - 1) // CHUNK

    items = lax.fori_loop(0, live_ref[0], one_pair, 0)
    for row in range(2):
        table_ref[row, slots] = 0
    for row in range(4):
        shift_ref[row, slots] = jnp.float32(0.0)
    for extra in range(BATCH - 1):
        item_ref[items + extra] = slots * steps
    count_ref[0] = (items + BATCH - 1) // BATCH


def work_list(extent, per_block, sizes, pair_list, pair_count):
    smem = pl.BlockSpec(memory_space=pltpu.SMEM)
    pairs = pair_list[0, 0, 0]
    slots = pairs.shape[1]
    steps = per_block // CHUNK
    return pl.pallas_call(
        functools.partial(work_kernel, extent[1:], per_block),
        out_shape=[
            jax.ShapeDtypeStruct(((slots + 1) * steps + BATCH,), jnp.int32),
            jax.ShapeDtypeStruct((2, slots + 1), jnp.int32),
            jax.ShapeDtypeStruct((4, slots + 1), jnp.float32),
            jax.ShapeDtypeStruct((1,), jnp.int32),
        ],
        in_specs=[smem] * 3,
        out_specs=[smem] * 4,
        compiler_params=pltpu.CompilerParams(vmem_limit_bytes=4 * 1024 * 1024),
    )(pairs, pair_count.reshape(1), sizes)


def sweep_kernel(force, adjoint, *refs):
    refs = list(refs)
    item_ref, table_ref, shift_ref, count_ref, pos_ref, par_ref = refs[:6]
    refs = refs[6:]
    cot_ref = refs.pop(0) if adjoint else None
    out_ref, state_ref, column_ref, row_ref, lane_ref = refs
    total, unused, per_block = pos_ref.shape
    rows_out = out_ref.shape[1]
    vectors = rows_out - 1 if adjoint else rows_out
    full = (CHUNK, per_block)
    steps = per_block // CHUNK

    for block in range(total):
        state_ref[block, 0:3, :] = pos_ref[block]
        state_ref[block, 3:7, :] = par_ref[block]
        if adjoint:
            state_ref[block, 8:11, :] = cot_ref[block]
    for block in range(total):
        column_ref[block] = state_ref[block].T

    def clear(block, carry):
        row_ref[block] = jnp.zeros((rows_out, per_block, per_block), jnp.float32)
        lane_ref[block] = jnp.zeros((rows_out, 8, per_block), jnp.float32)
        return carry

    lax.fori_loop(0, total, clear, 0)

    def item_terms(item):
        packed = item_ref[item]
        slot = packed // steps
        rows = table_ref[0, slot]
        lanes = table_ref[1, slot]
        start = pl.multiple_of((packed - slot * steps) * CHUNK, CHUNK)
        weight = shift_ref[3, slot]
        columns = column_ref[rows, pl.ds(start, CHUNK), :]

        def lane_row(part):
            return state_ref[lanes, part : part + 1, :]

        def row_column(part):
            return jnp.broadcast_to(columns[:, part : part + 1], full)

        lane_charge = lane_row(3) * (8.0 * weight)
        lane_depth = lane_row(5) * (24.0 * weight)
        d = [row_column(axis) - (lane_row(axis) - shift_ref[axis, slot]) for axis in range(3)]
        s = d[0] * d[0] + d[1] * d[1] + d[2] * d[2]
        sigma = row_column(4) + lane_row(4)
        square = sigma * sigma
        inverse = 1.0 / (s + square)
        t = square * inverse
        t3 = t * t * t
        soft = s + SOFT
        r = lax.rsqrt(soft)
        b = jnp.exp2(EXPONENT * (soft * r)) * r
        c = jnp.maximum(1.0 - s, 0.0)
        cc = c * c
        p = c * inverse
        y = c * r
        row_charge = row_column(3)
        et = row_column(5) * lane_depth * t3
        below = t3 - 1.0
        twice = t3 + below
        half = 1.0 + 0.5 * r
        k1 = 3.0 + y * half
        charge_b = lane_charge * b
        qb = row_charge * charge_b
        g1 = cc * (et * (below + p * twice) + qb * k1)
        row_terms = []
        if force:
            row_terms += [g1 * d[axis] for axis in range(3)]
        if adjoint:
            h = p * (p * (7.0 * t3 - 2.0) + 3.0 * twice) + below
            k2 = y * (y * (1.0 + r * (1.5 + 0.75 * r)) + 6.0 * half) + 6.0
            k = -2.0 * c * (2.0 * et * h + qb * k2)
            delta = [row_column(8 + axis) - lane_row(8 + axis) for axis in range(3)]
            along = delta[0] * d[0] + delta[1] * d[1] + delta[2] * d[2]
            ka = k * along
            row_terms += [g1 * delta[axis] + ka * d[axis] for axis in range(3)]

        def folded(value):
            return functools.reduce(
                lambda one, two: one + two,
                [value[8 * group : 8 * group + 8] for group in range(CHUNK // 8)],
            )

        lane_terms = [-folded(value) for value in row_terms]
        if adjoint:
            m = cc * k1 * along
            row_terms.append(m * charge_b)
            lane_terms.append(folded(m * b * row_charge) * (8.0 * weight))
        return (rows, lanes, start, row_terms, lane_terms)

    def one_batch(batch, carry):
        found = [item_terms(batch * BATCH + index) for index in range(BATCH)]
        for rows, lanes, start, row_terms, lane_terms in found:
            where = pl.ds(start, CHUNK)
            old_rows = [row_ref[rows, part, where, :] for part in range(rows_out)]
            old_lanes = [lane_ref[lanes, part] for part in range(rows_out)]
            for part in range(rows_out):
                row_ref[rows, part, where, :] = old_rows[part] + row_terms[part]
                lane_ref[lanes, part] = old_lanes[part] + lane_terms[part]
        return carry

    lax.fori_loop(0, count_ref[0], one_batch, 0)

    which = lax.broadcasted_iota(jnp.int32, (per_block, 8), 1)
    for block in range(total):
        columns = jnp.zeros((per_block, 8), jnp.float32)
        for part in range(rows_out):
            summed = jnp.sum(row_ref[block, part], axis=1, keepdims=True)
            columns = jnp.where(which == part, summed, columns)
        turned = columns.T
        sums = [jnp.sum(lane_ref[block, part], axis=0, keepdims=True) for part in range(rows_out)]
        out_ref[block] = turned[0:rows_out] + jnp.concatenate(sums, axis=0)


def sweep(ext_pos, ext_par, work, ext_cot, force):
    extent = ext_pos.shape[:3]
    per_block = ext_pos.shape[-1]
    total = extent[0] * extent[1] * extent[2]
    adjoint = ext_cot is not None
    rows_out = (3 if force else 0) + (4 if adjoint else 0)
    operands = list(work) + [ext_pos.reshape(total, 3, per_block), ext_par]
    if adjoint:
        operands.append(ext_cot.reshape(total, 3, per_block))
    smem = pl.BlockSpec(memory_space=pltpu.SMEM)
    vmem = pl.BlockSpec(memory_space=pltpu.VMEM)
    height = 16 if adjoint else 8
    out = pl.pallas_call(
        functools.partial(sweep_kernel, force, adjoint),
        out_shape=jax.ShapeDtypeStruct((total, rows_out, per_block), jnp.float32),
        in_specs=[smem] * 4 + [vmem] * (len(operands) - 4),
        out_specs=vmem,
        scratch_shapes=[
            pltpu.VMEM((total, height, per_block), jnp.float32),
            pltpu.VMEM((total, per_block, height), jnp.float32),
            pltpu.VMEM((total, rows_out, per_block, per_block), jnp.float32),
            pltpu.VMEM((total, rows_out, 8, per_block), jnp.float32),
        ],
        compiler_params=pltpu.CompilerParams(vmem_limit_bytes=40 * 1024 * 1024),
    )(*operands)
    return out.reshape(extent + (rows_out, per_block))


def on_device(
    positions,
    velocities,
    charges,
    atom_types,
    atom_count,
    sigma_type,
    epsilon_type,
    masses,
    pair_list,
    pair_count,
    pos_cotangent,
    vel_cotangent,
):
    alive_mask, params = atom_params(charges, atom_types, atom_count, sigma_type, epsilon_type)
    inverse = (1.0 / masses)[..., None, :]
    half_step = 0.5 * TIME_STEP
    own = positions.shape[:3]
    per_block = positions.shape[-1]
    half_scale = jnp.broadcast_to(half_step * inverse, positions.shape)
    full_scale = jnp.broadcast_to(TIME_STEP * inverse, positions.shape)
    field = jnp.concatenate([positions, params, half_scale * vel_cotangent], axis=3)
    (extended,) = exchange(first_kernel, 1, own, 0, [(True, 10)], field)
    ext_par = extended[:, :, :, 3:7].reshape(-1, 4, per_block)
    last_cot = extended[:, :, :, 7:10]
    sizes = jnp.sum(ext_par[:, 3], axis=-1).astype(jnp.int32)
    work = work_list(extended.shape[:3], per_block, sizes, pair_list, pair_count)
    history = [extended[:, :, :, :3]]
    velocity = velocities
    for step_index in range(STEPS):
        part = sweep(history[-1], ext_par, work, None, True)
        scale = half_scale if step_index == 0 else full_scale
        ext_next, velocity = exchange(
            forward_kernel, 2, own, 3, [(True, 3), (False, 3)], part, history[-1], velocity, scale
        )
        history.append(ext_next)
    part = sweep(history[STEPS], ext_par, work, last_cot, True)
    ext_cot, grad_position, grad_velocity, charge_sum, velocity = exchange(
        turn_kernel,
        3,
        own,
        7,
        [(True, 3), (False, 3), (False, 3), (False, 1), (False, 3)],
        part,
        velocity,
        half_scale,
        pos_cotangent,
        vel_cotangent,
        full_scale,
    )
    for step_index in range(STEPS - 1, 0, -1):
        part = sweep(history[step_index], ext_par, work, ext_cot, False)
        scale = full_scale if step_index > 1 else half_scale
        ext_cot, grad_position, grad_velocity, charge_sum = exchange(
            backward_kernel,
            4,
            own,
            4,
            [(True, 3), (False, 3), (False, 3), (False, 1)],
            part,
            grad_position,
            grad_velocity,
            scale,
            charge_sum,
        )
    part = sweep(history[0], ext_par, work, ext_cot, False)
    grad_position, charge_sum = exchange(
        last_kernel,
        5,
        own,
        4,
        [(False, 3), (False, 1)],
        part,
        grad_position,
        charge_sum,
        alive_mask[..., None, :],
    )
    position = history[STEPS][: own[0], : own[1], : own[2]]
    return (position, velocity, grad_position, grad_velocity, charge_sum[:, :, :, 0])


def solution(mesh):
    in_specs = (
        P("gx", "gy", "gz", None, None),
        P("gx", "gy", "gz", None, None),
        P("gx", "gy", "gz", None),
        P("gx", "gy", "gz", None),
        P("gx", "gy", "gz"),
        P(),
        P(),
        P("gx", "gy", "gz", None),
        P("gx", "gy", "gz", None, None),
        P("gx", "gy", "gz"),
        P("gx", "gy", "gz", None, None),
        P("gx", "gy", "gz", None, None),
    )
    out_specs = (
        P("gx", "gy", "gz", None, None),
        P("gx", "gy", "gz", None, None),
        P("gx", "gy", "gz", None, None),
        P("gx", "gy", "gz", None, None),
        P("gx", "gy", "gz", None),
    )
    return jax.shard_map(
        on_device, mesh=mesh, in_specs=in_specs, out_specs=out_specs, check_vma=False
    )
```
